256 devices in a mesh: section: 8 (over y, core), seq: 32 (over z, x).
Axes of the slice: x: 4, y: 4, z: 8, core: 2. Of those that a mesh axis runs over, the one named last changes fastest.
Arguments:
- inputs: bfloat16 [3, 1536, 2048], P(None, 'seq'), may hold values from -6 to 6
- norm_gain: bfloat16 [8, 2048], P('section'), may hold values from 0.25 to 1.75
- w_query: bfloat16 [8, 2048, 2048], P('section', 'seq')
- w_key: bfloat16 [8, 2048, 512], P('section', 'seq')
- w_value: bfloat16 [8, 2048, 512], P('section', 'seq'), may hold values from -0.125 to 0.125
- w_out: bfloat16 [8, 2048, 2048], P('section', 'seq'), may hold values from -0.125 to 0.125
Outputs:
- layer_outputs: bfloat16 [8, 3, 1536, 2048], P('section', None, 'seq')
The draws below stay inside these ranges and needn't reach their ends.
All inputs are finite; a program needn't handle non-finite values.
Results may differ from the reference program's by a relative error of at most 0.04.
Values may be sent and summed in bfloat16 or wider, within the bound.
No kernel may reach another device: no remote copies, remote signals or barrier semaphores. Data moves between devices by JAX's collectives and lax.ppermute only.
A program may use at most 64 MiB of HBM per device.

```python
import jax
import jax.numpy as jnp
from jax import lax

D = 2048
HEADS = 32
KVH = 8
HD = 64
MICRO = 3
LAYERS = 8
SPAN = 1536
SEQLEN = 4608


def key_base(key):
    return jax.random.normal(jax.random.fold_in(key, 101), (LAYERS, D, KVH * HD), jnp.float32) * D ** (-0.5)


def draw_w_key(key, part):
    return key_base(key).astype(jnp.bfloat16)


def draw_w_query(key, part):
    own_part = jax.random.normal(jax.random.fold_in(key, 202), (LAYERS, D, HEADS * HD), jnp.float32) * (2.0 * D ** (-0.5))
    return own_part.astype(jnp.bfloat16)


def steps_of(key, shape, shards, least, top_value):
    loudness, own = 1.0, jax.random.fold_in(key, 6)
    for position, shards_of in shards:
        draws = jnp.exp(jax.random.uniform(jax.random.fold_in(own, position), (shards_of,), jnp.float32, least / len(shards), top_value / len(shards)))
        loudness = loudness * jnp.repeat(draws, shape[position] // shards_of).reshape([-1 if axis == position else 1 for axis in range(len(shape))])
    return loudness


def centred(own_key, shape, spread, most, cuts=(), kind=jnp.bfloat16):
    array = jax.random.normal(own_key, shape, jnp.float32) * spread
    if len(cuts) > 0:
        array = steps_of(own_key, shape, cuts, -0.22, 0.18) * array
    return jnp.clip(array, min=-most, max=most).astype(kind)


def setup_inputs(seed: int = 0) -> dict:
    key_list = jax.random.split(jax.random.key(seed), 7)
    return {
        "inputs": centred(key_list[0], (MICRO, SPAN, D), 1.0, 6.0, ((1, 32),)),
        "norm_gain": jnp.clip(1.0 + 0.15 * jax.random.normal(key_list[1], (LAYERS, D), jnp.float32), 0.25, 1.75).astype(jnp.bfloat16),
        "w_query": draw_w_query(jax.random.fold_in(key_list[6], 71), 0),
        "w_key": draw_w_key(jax.random.fold_in(key_list[6], 71), 0),
        "w_value": centred(key_list[4], (LAYERS, D, KVH * HD), D ** -0.5, 0.125, ((0, 8), (1, 32))),
        "w_out": centred(key_list[5], (LAYERS, HEADS * HD, D), (HEADS * HD) ** -0.5, 0.125, ((0, 8), (1, 32))),
    }


epsilon = 1e-05

def head_attention(operands):
    head_queries, head_keys, head_values = operands
    scores = jnp.dot(head_queries, head_keys.T, preferred_element_type=jnp.float32) * HD ** (-0.5)
    positions = jnp.arange(SEQLEN, dtype=jnp.int32)
    visible = positions[None, :] <= positions[:, None]
    scores = jnp.where(visible, scores, jnp.float32(-1e+30))
    peak = lax.optimization_barrier(jnp.max(scores, axis=-1, keepdims=True))
    probs = jnp.exp(scores - peak)
    total = lax.optimization_barrier(jnp.sum(probs, axis=-1, keepdims=True))
    summed = jnp.dot(probs.astype(jnp.bfloat16), head_values, preferred_element_type=jnp.float32)
    return (summed / total).astype(jnp.bfloat16)

def reference(inputs, norm_gain, w_query, w_key, w_value, w_out):
    hidden = inputs.reshape(SEQLEN, D)
    results = []
    share_count = HEADS // KVH
    for layer_id in range(LAYERS):
        wide_rows = hidden.astype(jnp.float32)
        scale_rows = lax.rsqrt(lax.optimization_barrier(jnp.mean(wide_rows * wide_rows, axis=-1, keepdims=True)) + epsilon)
        normed_rows = (wide_rows * scale_rows * norm_gain[layer_id].astype(jnp.float32)).astype(jnp.bfloat16)
        queries = jnp.dot(normed_rows, w_query[layer_id], preferred_element_type=jnp.float32).astype(jnp.bfloat16)
        keys = jnp.dot(normed_rows, w_key[layer_id], preferred_element_type=jnp.float32).astype(jnp.bfloat16)
        values = jnp.dot(normed_rows, w_value[layer_id], preferred_element_type=jnp.float32).astype(jnp.bfloat16)
        query_heads = queries.reshape(SEQLEN, HEADS, HD).transpose(1, 0, 2)
        key_heads = jnp.repeat(keys.reshape(SEQLEN, KVH, HD).transpose(1, 0, 2), share_count, axis=0)
        value_heads = jnp.repeat(values.reshape(SEQLEN, KVH, HD).transpose(1, 0, 2), share_count, axis=0)
        attended = lax.map(head_attention, (query_heads, key_heads, value_heads))
        attended = attended.transpose(1, 0, 2).reshape(SEQLEN, HEADS * HD)
        update = jnp.dot(attended, w_out[layer_id], preferred_element_type=jnp.float32)
        hidden = (hidden.astype(jnp.float32) + update).astype(jnp.bfloat16)
        results.append(hidden.reshape(MICRO, SPAN, D))
    return jnp.stack(results)
```

```python
import functools

import jax
import jax.numpy as jnp
from jax import lax
from jax.experimental import pallas as pl
from jax.experimental.pallas import tpu as pltpu
from jax.sharding import PartitionSpec as P

HEADS = 32
KVH = 8
HD = 64
SHARE = HEADS // KVH
QW = SHARE * HD
EPS = 1e-05
NEG = -1e30

ZN = 8
XN = 4
SN = 8
F32 = jnp.float32
BF16 = jnp.bfloat16


def seq_pairs(mask):
    return [(i, i ^ mask) for i in range(ZN * XN)]


def section_pairs(mask):
    return [(i, i ^ mask) for i in range(SN)]


def along_z():
    return [[z * XN + x for z in range(ZN)] for x in range(XN)]


def spread(piece):
    near = [piece] + [lax.ppermute(piece, "section", section_pairs(2 * d)) for d in (1, 2, 3)]
    other = lax.ppermute(jnp.stack(near), "section", section_pairs(1))
    return near + [other]


def in_order(refs):
    out = [(2 * d, refs[d][...]) for d in range(4)]
    out += [(2 * d + 1, refs[4][d]) for d in range(4)]
    return out


def project_kernel(me_ref, gain_ref, p0, p1, p2, p3, p4, wq_ref, wkv_ref, q_ref, kv_ref):
    me = me_ref[0]
    pieces = [(mask, value.astype(F32)) for mask, value in in_order([p0, p1, p2, p3, p4])]
    rows = pieces[0][1].shape[0]
    width = sum(value.shape[1] for _, value in pieces)
    squares = functools.reduce(jnp.add, [value * value for _, value in pieces])
    scale = lax.rsqrt(jnp.sum(squares, axis=-1, keepdims=True) / width + EPS)
    q_sum = jnp.zeros((rows, QW), F32)
    kv_sum = jnp.zeros((rows, 2 * HD), F32)
    for mask, value in pieces:
        owner = jnp.bitwise_xor(me, mask)
        gain = gain_ref[pl.ds(owner, 1), 0, :].astype(F32)
        normed = (value * scale * gain).astype(BF16)
        wq = wq_ref[pl.ds(4 * owner, 4), 0].reshape(QW, QW)
        wkv = wkv_ref[pl.ds(4 * owner, 4), 0].reshape(QW, 2 * HD)
        q_sum += jnp.dot(normed, wq, preferred_element_type=F32)
        kv_sum += jnp.dot(normed, wkv, preferred_element_type=F32)
    q_ref[...] = q_sum.astype(BF16)
    pair = kv_sum.astype(BF16)
    for i in range(kv_ref.shape[0]):
        kv_ref[i] = pair


def attend_kernel(seq_ref, q_ref, k0, k1, k2, k3, o_ref, *, blocks, tok):
    seq = seq_ref[0]
    x_me = jnp.bitwise_and(seq, XN - 1)
    keys = [k0, k1, k2, k3]
    span = ZN * tok
    rows = SHARE * tok
    q_all = q_ref[...]
    row_pos = lax.broadcasted_iota(jnp.int32, (rows, span), 0)
    row_pos = seq * tok + lax.rem(row_pos, tok)
    col = lax.broadcasted_iota(jnp.int32, (rows, span), 1)
    col_pos = lax.div(col, tok) * (XN * tok) + lax.rem(col, tok)
    slack = row_pos - col_pos
    factor = HD**-0.5
    for b in range(blocks):
        q_rows = q_all[b * tok : (b + 1) * tok]
        q_heads = jnp.concatenate([q_rows[:, h * HD : (h + 1) * HD] for h in range(SHARE)], axis=0)
        q_heads = jnp.concatenate([q_heads, jnp.zeros((rows, HD), BF16)], axis=1)
        scores = []
        for kb in range(b + 1):
            for d in range(XN):
                pair = keys[d][:, kb * tok : (kb + 1) * tok, :].reshape(span, 2 * HD)
                s = lax.dot_general(q_heads, pair, (((1,), (1,)), ((), ())), preferred_element_type=F32)
                if kb == b:
                    offset = jnp.bitwise_xor(x_me, d) * tok
                    s = jnp.where(slack >= offset, s, NEG)
                scores.append((kb, d, s))
        peak = functools.reduce(jnp.maximum, [s for _, _, s in scores])
        peak = jnp.max(peak, axis=-1, keepdims=True)
        total = jnp.zeros((rows, span), F32)
        summed = jnp.zeros((rows, 2 * HD), F32)
        for kb, d, s in scores:
            probs = jnp.exp((s - peak) * factor)
            total += probs
            pair = keys[d][:, kb * tok : (kb + 1) * tok, :].reshape(span, 2 * HD)
            summed += jnp.dot(probs.astype(BF16), pair, preferred_element_type=F32)
        total = jnp.sum(total, axis=-1, keepdims=True)
        result = (summed[:, HD:] / total).astype(BF16)
        o_ref[b * tok : (b + 1) * tok, :] = jnp.concatenate(
            [result[h * tok : (h + 1) * tok] for h in range(SHARE)], axis=1
        )


def output_kernel(me_ref, a0, a1, a2, a3, a4, h_ref, w_ref, o_ref):
    me = me_ref[0]
    total = h_ref[...].astype(F32)
    update = jnp.zeros(total.shape, F32)
    for mask, value in in_order([a0, a1, a2, a3, a4]):
        owner = jnp.bitwise_xor(me, mask)
        w = w_ref[pl.ds(4 * owner, 4), 0].reshape(QW, QW)
        update += jnp.dot(value, w, preferred_element_type=F32)
    o_ref[...] = (total + update).astype(BF16)


SMEM = pl.BlockSpec(memory_space=pltpu.SMEM)


def whole(shape):
    return pl.BlockSpec(shape, lambda i: (0,) * len(shape))


def call(kernel, out_shape, in_specs, flops, bytes_accessed, exps=0):
    if isinstance(out_shape, list):
        out_specs = [whole(o.shape) for o in out_shape]
    else:
        out_specs = whole(out_shape.shape)
    return pl.pallas_call(
        kernel,
        out_shape=out_shape,
        grid=(1,),
        in_specs=in_specs,
        out_specs=out_specs,
        compiler_params=pltpu.CompilerParams(vmem_limit_bytes=48 * 1024 * 1024),
        cost_estimate=pl.CostEstimate(flops=flops, bytes_accessed=bytes_accessed, transcendentals=exps),
    )


def local(inputs, norm_gain, w_query, w_key, w_value, w_out):
    blocks, tok, width = inputs.shape
    rows = blocks * tok
    me = lax.axis_index("section")
    seq = lax.axis_index("seq")
    me_s = me.reshape(1)
    seq_s = seq.reshape(1)
    layers = lax.axis_size("section")
    shard = w_query.shape[1]

    def cut(w):
        return w[0].reshape(shard, SN, -1).transpose(1, 0, 2)

    mine = jnp.concatenate([cut(w_query), cut(w_out), cut(w_key), cut(w_value)], axis=-1)
    by_layer = lax.all_to_all(mine, "section", split_axis=0, concat_axis=0, tiled=True)
    weights = lax.all_gather(by_layer, "seq", axis=0)
    gains = lax.all_gather(norm_gain, "section", axis=0, tiled=True).reshape(layers, SN, 1, QW)

    flat = inputs.reshape(rows, width)

    def input_piece(mask):
        return lax.dynamic_slice_in_dim(flat, jnp.bitwise_xor(me, mask) * QW, QW, 1)

    pieces = [input_piece(2 * d) for d in range(4)]
    pieces.append(jnp.stack([input_piece(2 * d + 1) for d in range(4)]))

    piece_specs = [whole((rows, QW))] * 4 + [whole((4, rows, QW))]
    kv_shape = (ZN, rows, 2 * HD)
    results = []
    for layer in range(layers):

        def weight_spec(width_, index, layer=layer):
            return pl.BlockSpec((ZN * XN, 1, shard, width_), lambda i: (0, layer, 0, index))

        with jax.named_scope("project"):
            q, kv = call(
                project_kernel,
                [
                    jax.ShapeDtypeStruct((rows, QW), BF16),
                    jax.ShapeDtypeStruct(kv_shape, BF16),
                ],
                [SMEM, whole((SN, 1, QW))] + piece_specs + [weight_spec(QW, 0), weight_spec(2 * HD, 4)],
                2 * rows * width * 384,
                2 * (width * 384 + rows * width),
            )(me_s, gains[layer], *pieces, weights, weights)
        with jax.named_scope("keys"):
            kv0 = lax.all_to_all(
                kv, "seq", split_axis=0, concat_axis=0, tiled=True, axis_index_groups=along_z()
            )
            kvs = [kv0] + [lax.ppermute(kv0, "seq", seq_pairs(d)) for d in (1, 2, 3)]
        with jax.named_scope("attend"):
            attended = call(
                functools.partial(attend_kernel, blocks=blocks, tok=tok),
                jax.ShapeDtypeStruct((rows, QW), BF16),
                [SMEM, whole((rows, QW))] + [whole(kv_shape)] * 4,
                4 * SHARE * tok * (ZN * XN * tok) * 128 * 6,
                4 * 2 * ZN * rows * 128,
                SHARE * tok * (ZN * XN * tok) * 6,
            )(seq_s, q, *kvs)
            heads = spread(attended)
        with jax.named_scope("output"):
            own = call(
                output_kernel,
                jax.ShapeDtypeStruct((rows, QW), BF16),
                [SMEM] + piece_specs + [whole((rows, QW)), weight_spec(QW, 1)],
                2 * rows * width * QW,
                2 * (width * QW + rows * width),
            )(me_s, *heads, pieces[0], weights)
            pieces = spread(own)
        results.append(pieces)

    def pick(layer):
        def branch(all_pieces):
            near, other = all_pieces[layer][:4], all_pieces[layer][4]
            parts = []
            for s in range(SN):
                mask = s ^ layer
                parts.append(other[mask // 2] if mask % 2 else near[mask // 2])
            return jnp.concatenate(parts, axis=1)

        return branch

    chosen = lax.switch(me, [pick(layer) for layer in range(layers)], results)
    return chosen.reshape(1, blocks, tok, width)


def solution(mesh):
    in_specs = (
        P(None, "seq", None),
        P("section", None),
        P("section", "seq", None),
        P("section", "seq", None),
        P("section", "seq", None),
        P("section", "seq", None),
    )
    out_specs = P("section", None, "seq", None)
    return jax.shard_map(local, mesh=mesh, in_specs=in_specs, out_specs=out_specs, check_vma=False)
```

```python
import functools

import jax
import jax.numpy as jnp
from jax import lax
from jax.experimental import pallas as pl
from jax.experimental.pallas import tpu as pltpu
from jax.sharding import PartitionSpec as P

HEADS = 32
KVH = 8
HD = 64
SHARE = HEADS // KVH
QW = SHARE * HD
EPS = 1e-05
NEG = -1e30

ZN = 8
XN = 4
SN = 8
F32 = jnp.float32
BF16 = jnp.bfloat16


def seq_pairs(mask):
    return [(i, i ^ mask) for i in range(ZN * XN)]


def section_pairs(mask):
    return [(i, i ^ mask) for i in range(SN)]


def along_z():
    return [[z * XN + x for z in range(ZN)] for x in range(XN)]


def spread(piece):
    near = [piece] + [lax.ppermute(piece, "section", section_pairs(2 * d)) for d in (1, 2, 3)]
    other = lax.ppermute(jnp.stack(near), "section", section_pairs(1))
    return near + [other]


def in_order(refs):
    out = [(2 * d, refs[d][...]) for d in range(4)]
    out += [(2 * d + 1, refs[4][d]) for d in range(4)]
    return out


def project(me, gain_ref, piece_refs, w_of, q_ref, kv_ref):
    pieces = [(mask, value.astype(F32)) for mask, value in in_order(piece_refs)]
    rows = pieces[0][1].shape[0]
    width = sum(value.shape[1] for _, value in pieces)
    squares = functools.reduce(jnp.add, [value * value for _, value in pieces])
    scale = lax.rsqrt(jnp.sum(squares, axis=-1, keepdims=True) / width + EPS)
    q_sum = jnp.zeros((rows, QW), F32)
    kv_sum = jnp.zeros((rows, 2 * HD), F32)
    for mask, value in pieces:
        owner = jnp.bitwise_xor(me, mask)
        gain = gain_ref[pl.ds(owner, 1), 0, :].astype(F32)
        normed = (value * scale * gain).astype(BF16)
        wq, wkv = w_of(owner)
        q_sum += jnp.dot(normed, wq, preferred_element_type=F32)
        kv_sum += jnp.dot(normed, wkv, preferred_element_type=F32)
    q_ref[...] = q_sum.astype(BF16)
    pair = kv_sum.astype(BF16)
    for i in range(kv_ref.shape[0]):
        kv_ref[i] = pair


def project_kernel(me_ref, gain_ref, p0, p1, p2, p3, p4, wq_ref, wkv_ref, q_ref, kv_ref):
    def w_of(owner):
        wq = wq_ref[pl.ds(XN * owner, XN), 0].reshape(QW, QW)
        wkv = wkv_ref[pl.ds(XN * owner, XN), 0].reshape(QW, 2 * HD)
        return wq, wkv

    project(me_ref[0], gain_ref, [p0, p1, p2, p3, p4], w_of, q_ref, kv_ref)


def assemble(seq, parts, held):
    x_me = jnp.bitwise_and(seq, XN - 1)
    for d in range(XN):
        held[jnp.bitwise_xor(x_me, d)] = parts[d][...]


def first_project_kernel(
    me_ref, seq_ref, gain_ref, p0, p1, p2, p3, p4, w0, w1, w2, w3, q_ref, kv_ref, held
):
    assemble(seq_ref[0], [w0, w1, w2, w3], held)

    def w_of(owner):
        w = held[:, owner].reshape(QW, QW + 2 * HD)
        return w[:, :QW], w[:, QW:]

    project(me_ref[0], gain_ref, [p0, p1, p2, p3, p4], w_of, q_ref, kv_ref)


def attend_kernel(seq_ref, q0, q1, q2, q3, k_ref, o0, o1, o2, o3, q_held, o_held, *, blocks, tok):
    seq = seq_ref[0]
    x_me = jnp.bitwise_and(seq, XN - 1)
    span = ZN * tok
    rows = SHARE * tok
    for d, q_ref in enumerate([q0, q1, q2, q3]):
        q_held[d] = q_ref[...]
    row = lax.broadcasted_iota(jnp.int32, (rows, span), 0)
    col = lax.broadcasted_iota(jnp.int32, (rows, span), 1)
    slack = lax.rem(row, tok) - lax.div(col, tok) * (XN * tok) - lax.rem(col, tok)
    lane = lax.broadcasted_iota(jnp.int32, (tok, 2 * HD), 1)
    factor = HD**-0.5

    @pl.loop(0, XN)
    def _(d):
        asker = seq - x_me + jnp.bitwise_xor(x_me, d)
        visible = slack >= (x_me - asker) * tok
        for b in range(blocks):
            q_rows = q_held[d, b * tok : (b + 1) * tok]
            q_heads = jnp.concatenate([q_rows[:, h * HD : (h + 1) * HD] for h in range(SHARE)], axis=0)
            q_heads = jnp.concatenate([q_heads, jnp.zeros((rows, HD), BF16)], axis=1)
            scores = []
            pairs = []
            for kb in range(b + 1):
                pair = k_ref[:, kb * tok : (kb + 1) * tok, :].reshape(span, 2 * HD)
                s = lax.dot_general(q_heads, pair, (((1,), (1,)), ((), ())), preferred_element_type=F32)
                if kb == b:
                    s = jnp.where(visible, s, NEG)
                scores.append(s)
                pairs.append(pair)
            peak = jnp.max(functools.reduce(jnp.maximum, scores), axis=-1, keepdims=True)
            total = jnp.zeros((rows, span), F32)
            summed = jnp.zeros((rows, 2 * HD), F32)
            for s, pair in zip(scores, pairs):
                probs = jnp.exp((s - peak) * factor)
                total += probs
                summed += jnp.dot(probs.astype(BF16), pair, preferred_element_type=F32)
            total = jnp.sum(total, axis=-1, keepdims=True)
            result = (summed[:, HD:] / total).astype(BF16)
            weight = peak * factor + jnp.log(total)
            high = weight.astype(BF16).astype(F32)
            low = weight - high
            notes = jnp.zeros((tok, 2 * HD), F32)
            for h in range(SHARE):
                part = slice(h * tok, (h + 1) * tok)
                notes = jnp.where(lane == h, high[part], notes)
                notes = jnp.where(lane == SHARE + h, low[part], notes)
            o_held[d, b * tok : (b + 1) * tok, :] = jnp.concatenate(
                [result[h * tok : (h + 1) * tok] for h in range(SHARE)] + [notes.astype(BF16)], axis=1
            )

    for d, o_ref in enumerate([o0, o1, o2, o3]):
        o_ref[...] = o_held[d]


def combine_kernel(o0, o1, o2, o3, a_ref):
    parts = [o0[...], o1[...], o2[...], o3[...]]
    notes = [part[:, QW:].astype(F32) for part in parts]
    for h in range(SHARE):
        weights = [n[:, h : h + 1] + n[:, SHARE + h : SHARE + h + 1] for n in notes]
        peak = functools.reduce(jnp.maximum, weights)
        weights = [jnp.exp(w - peak) for w in weights]
        total = functools.reduce(jnp.add, weights)
        cols = slice(h * HD, (h + 1) * HD)
        mixed = functools.reduce(
            jnp.add, [w / total * part[:, cols].astype(F32) for w, part in zip(weights, parts)]
        )
        a_ref[:, cols] = mixed.astype(BF16)


def output(me, piece_refs, h_ref, w_of, o_ref):
    total = h_ref[...].astype(F32)
    update = jnp.zeros(total.shape, F32)
    for mask, value in in_order(piece_refs):
        update += jnp.dot(value, w_of(jnp.bitwise_xor(me, mask)), preferred_element_type=F32)
    o_ref[...] = (total + update).astype(BF16)


def output_kernel(me_ref, a0, a1, a2, a3, a4, h_ref, w_ref, o_ref):
    def w_of(owner):
        return w_ref[pl.ds(XN * owner, XN), 0].reshape(QW, QW)

    output(me_ref[0], [a0, a1, a2, a3, a4], h_ref, w_of, o_ref)


def first_output_kernel(me_ref, seq_ref, a0, a1, a2, a3, a4, h_ref, w0, w1, w2, w3, o_ref, held):
    assemble(seq_ref[0], [w0, w1, w2, w3], held)
    output(me_ref[0], [a0, a1, a2, a3, a4], h_ref, lambda owner: held[:, owner].reshape(QW, QW), o_ref)


SMEM = pl.BlockSpec(memory_space=pltpu.SMEM)


def whole(shape):
    return pl.BlockSpec(shape, lambda i: (0,) * len(shape))


def call(kernel, out_shape, in_specs, flops, bytes_accessed, exps=0, scratch=()):
    if isinstance(out_shape, list):
        out_specs = [whole(o.shape) for o in out_shape]
    else:
        out_specs = whole(out_shape.shape)
    return pl.pallas_call(
        kernel,
        out_shape=out_shape,
        grid=(1,),
        in_specs=in_specs,
        out_specs=out_specs,
        scratch_shapes=list(scratch),
        compiler_params=pltpu.CompilerParams(vmem_limit_bytes=48 * 1024 * 1024),
        cost_estimate=pl.CostEstimate(flops=flops, bytes_accessed=bytes_accessed, transcendentals=exps),
    )


def local(inputs, norm_gain, w_query, w_key, w_value, w_out):
    blocks, tok, width = inputs.shape
    rows = blocks * tok
    me = lax.axis_index("section")
    seq = lax.axis_index("seq")
    me_s = me.reshape(1)
    seq_s = seq.reshape(1)
    layers = lax.axis_size("section")
    shard = w_query.shape[1]
    qkv_w = QW + 2 * HD
    all_w = QW + qkv_w

    def cut(w):
        return w[0].reshape(shard, SN, -1).transpose(1, 0, 2)

    gain_rows = jnp.pad(norm_gain.reshape(4, width // 4), ((0, 12), (0, all_w - width // 4)))
    mine = jnp.concatenate([cut(w_query), cut(w_out), cut(w_key), cut(w_value)], axis=-1)
    mine = jnp.concatenate([mine, jnp.broadcast_to(gain_rows[None], (SN, 16, all_w))], axis=1)
    by_layer = lax.all_to_all(mine, "section", split_axis=0, concat_axis=0, tiled=True)
    gains = by_layer[:, shard : shard + 4, : width // 4].reshape(layers, SN, 1, QW)

    with jax.named_scope("weights"):
        early = lax.all_gather(by_layer[1:4, :shard], "seq", axis=0)
        late = lax.all_gather(by_layer[4:, :shard], "seq", axis=0)
        first = jnp.broadcast_to(by_layer[None, 0, :shard], (ZN, shard, all_w))
        first = lax.all_to_all(
            first, "seq", split_axis=0, concat_axis=0, tiled=True, axis_index_groups=along_z()
        )
        first_qkv = jnp.concatenate([first[:, :, :QW], first[:, :, 2 * QW :]], axis=-1)
        first_out = first[:, :, QW : 2 * QW]
        first_qkv = [first_qkv] + [lax.ppermute(first_qkv, "seq", seq_pairs(d)) for d in (1, 2, 3)]
        first_out = [first_out] + [lax.ppermute(first_out, "seq", seq_pairs(d)) for d in (1, 2, 3)]

    flat = inputs.reshape(rows, width)

    def input_piece(mask):
        return lax.dynamic_slice_in_dim(flat, jnp.bitwise_xor(me, mask) * QW, QW, 1)

    pieces = [input_piece(2 * d) for d in range(4)]
    pieces.append(jnp.stack([input_piece(2 * d + 1) for d in range(4)]))

    piece_shape = jax.ShapeDtypeStruct((rows, QW), BF16)
    piece_specs = [whole((rows, QW))] * 4 + [whole((4, rows, QW))]
    kv_shape = (ZN, rows, 2 * HD)
    part_shape = (rows, QW + 2 * HD)
    seq_keys = ZN * XN * tok
    results = []
    for layer in range(layers):
        group, slot = (early, layer - 1) if layer < 4 else (late, layer - 4)

        def weight_spec(width_, index, slot=slot):
            return pl.BlockSpec((ZN * XN, 1, shard, width_), lambda i: (0, slot, 0, index))

        with jax.named_scope("project"):
            outs = [piece_shape, jax.ShapeDtypeStruct(kv_shape, BF16)]
            cost = (2 * rows * width * qkv_w, 2 * (width * qkv_w + rows * width))
            if layer == 0:
                q, kv = call(
                    first_project_kernel,
                    outs,
                    [SMEM, SMEM, whole((SN, 1, QW))] + piece_specs + [whole((ZN, shard, qkv_w))] * 4,
                    *cost,
                    scratch=[pltpu.VMEM((XN, ZN, shard, qkv_w), BF16)],
                )(me_s, seq_s, gains[layer], *pieces, *first_qkv)
            else:
                q, kv = call(
                    project_kernel,
                    outs,
                    [SMEM, whole((SN, 1, QW))] + piece_specs + [weight_spec(QW, 0), weight_spec(2 * HD, 4)],
                    *cost,
                )(me_s, gains[layer], *pieces, group, group)
        with jax.named_scope("exchange"):
            qs = [q] + [lax.ppermute(q, "seq", seq_pairs(d)) for d in (1, 2, 3)]
            kv = lax.all_to_all(
                kv, "seq", split_axis=0, concat_axis=0, tiled=True, axis_index_groups=along_z()
            )
        with jax.named_scope("attend"):
            parts = call(
                functools.partial(attend_kernel, blocks=blocks, tok=tok),
                [jax.ShapeDtypeStruct(part_shape, BF16)] * XN,
                [SMEM] + [whole((rows, QW))] * XN + [whole(kv_shape)],
                4 * SHARE * tok * seq_keys * 128 * 6,
                2 * (ZN * rows * 128 + 10 * rows * QW),
                SHARE * tok * seq_keys * 6,
                scratch=[pltpu.VMEM((XN, rows, QW), BF16), pltpu.VMEM((XN,) + part_shape, BF16)],
            )(seq_s, *qs, kv)
            parts = [parts[0]] + [lax.ppermute(parts[d], "seq", seq_pairs(d)) for d in (1, 2, 3)]
            attended = call(
                combine_kernel,
                piece_shape,
                [whole(part_shape)] * XN,
                10 * rows * QW,
                10 * rows * QW,
            )(*parts)
            heads = spread(attended)
        with jax.named_scope("output"):
            cost = (2 * rows * width * QW, 2 * (width * QW + rows * width))
            if layer == 0:
                own = call(
                    first_output_kernel,
                    piece_shape,
                    [SMEM, SMEM] + piece_specs + [whole((rows, QW))] + [whole((ZN, shard, QW))] * 4,
                    *cost,
                    scratch=[pltpu.VMEM((XN, ZN, shard, QW), BF16)],
                )(me_s, seq_s, *heads, pieces[0], *first_out)
            else:
                own = call(
                    output_kernel,
                    piece_shape,
                    [SMEM] + piece_specs + [whole((rows, QW)), weight_spec(QW, 1)],
                    *cost,
                )(me_s, *heads, pieces[0], group)
            pieces = spread(own)
        results.append(pieces)

    def pick(layer):
        def branch(all_pieces):
            near, other = all_pieces[layer][:4], all_pieces[layer][4]
            parts = []
            for s in range(SN):
                mask = s ^ layer
                parts.append(other[mask // 2] if mask % 2 else near[mask // 2])
            return jnp.concatenate(parts, axis=1)

        return branch

    chosen = lax.switch(me, [pick(layer) for layer in range(layers)], results)
    return chosen.reshape(1, blocks, tok, width)


def solution(mesh):
    in_specs = (
        P(None, "seq", None),
        P("section", None),
        P("section", "seq", None),
        P("section", "seq", None),
        P("section", "seq", None),
        P("section", "seq", None),
    )
    out_specs = P("section", None, "seq", None)
    return jax.shard_map(local, mesh=mesh, in_specs=in_specs, out_specs=out_specs, check_vma=False)
```

```python
import functools

import jax
import jax.numpy as jnp
from jax import lax
from jax.experimental import pallas as pl
from jax.experimental.pallas import tpu as pltpu
from jax.sharding import PartitionSpec as P

HEADS = 32
KVH = 8
HD = 64
SHARE = HEADS // KVH
QW = SHARE * HD
EPS = 1e-05
NEG = -1e30
LOG2E = 1.4426950408889634
LOOPED = True

ZN = 8
XN = 4
SN = 8
F32 = jnp.float32
BF16 = jnp.bfloat16


def seq_pairs(mask):
    return [(i, i ^ mask) for i in range(ZN * XN)]


def section_pairs(mask):
    return [(i, i ^ mask) for i in range(SN)]


def along_z():
    return [[z * XN + x for z in range(ZN)] for x in range(XN)]


def spread(piece):
    near = [piece] + [lax.ppermute(piece, "section", section_pairs(2 * d)) for d in (1, 2, 3)]
    other = lax.ppermute(jnp.stack(near), "section", section_pairs(1))
    return near + [other]


def in_order(refs):
    out = [(2 * d, refs[d][...]) for d in range(4)]
    out += [(2 * d + 1, refs[4][d]) for d in range(4)]
    return out


def place(me, layer, piece_refs, out_ref, sems):
    def copies():
        for i, (mask, source) in enumerate(sources(piece_refs)):
            first = pl.multiple_of(jnp.bitwise_xor(me, mask) * QW, QW)
            yield pltpu.make_async_copy(source, out_ref.at[:, pl.ds(first, QW)], sems.at[i])

    @pl.when(me == layer - 1)
    def _():
        for copy in copies():
            copy.start()
        for copy in copies():
            copy.wait()


def sources(refs):
    out = [(2 * d, refs[d]) for d in range(4)]
    return out + [(2 * d + 1, refs[4].at[d]) for d in range(4)]


def place_kernel(scal, p0, p1, p2, p3, p4, out_in, out_ref, sems):
    place(scal[0], scal[3], [p0, p1, p2, p3, p4], out_ref, sems)


def project(me, gain_ref, piece_refs, w_of, q_ref, kv_ref):
    pieces = [(mask, value.astype(F32)) for mask, value in in_order(piece_refs)]
    rows = pieces[0][1].shape[0]
    width = sum(value.shape[1] for _, value in pieces)
    squares = functools.reduce(jnp.add, [value * value for _, value in pieces])
    scale = lax.rsqrt(jnp.sum(squares, axis=-1, keepdims=True) / width + EPS)
    q_sum = jnp.zeros((rows, QW), F32)
    kv_sum = jnp.zeros((rows, 2 * HD), F32)
    for mask, value in pieces:
        owner = jnp.bitwise_xor(me, mask)
        gain = gain_ref[0, pl.ds(owner, 1), 0, :].astype(F32)
        normed = (value * scale * gain).astype(BF16)
        wq, wkv = w_of(owner)
        q_sum += jnp.dot(normed, wq, preferred_element_type=F32)
        kv_sum += jnp.dot(normed, wkv, preferred_element_type=F32)
    q_ref[...] = q_sum.astype(BF16)
    pair = kv_sum.astype(BF16)
    for i in range(kv_ref.shape[0]):
        kv_ref[i] = pair


def project_kernel(
    scal, gain_ref, p0, p1, p2, p3, p4, wq_ref, wkv_ref, out_in, q_ref, kv_ref, out_ref, sems
):
    def w_of(owner):
        wq = wq_ref[pl.ds(XN * owner, XN), 0].reshape(QW, QW)
        wkv = wkv_ref[pl.ds(XN * owner, XN), 0].reshape(QW, 2 * HD)
        return wq, wkv

    refs = [p0, p1, p2, p3, p4]
    project(scal[0], gain_ref, refs, w_of, q_ref, kv_ref)
    place(scal[0], scal[3], refs, out_ref, sems)


def assemble(seq, parts, held):
    x_me = jnp.bitwise_and(seq, XN - 1)
    for d in range(XN):
        held[jnp.bitwise_xor(x_me, d)] = parts[d][...]


def first_project_kernel(
    scal, gain_ref, p0, p1, p2, p3, p4, w0, w1, w2, w3, q_ref, kv_ref, held
):
    assemble(scal[1], [w0, w1, w2, w3], held)

    def w_of(owner):
        w = held[:, owner].reshape(QW, QW + 2 * HD)
        return w[:, :QW], w[:, QW:]

    project(scal[0], gain_ref, [p0, p1, p2, p3, p4], w_of, q_ref, kv_ref)


def attend_kernel(scal, q_ref, k_ref, o_ref, *, d, blocks, tok):
    seq = scal[1]
    x_me = jnp.bitwise_and(seq, XN - 1)
    span = ZN * tok
    rows = SHARE * tok
    row = lax.broadcasted_iota(jnp.int32, (rows, span), 0)
    col = lax.broadcasted_iota(jnp.int32, (rows, span), 1)
    slack = lax.rem(row, tok) - lax.div(col, tok) * (XN * tok) - lax.rem(col, tok)
    asker = seq - x_me + jnp.bitwise_xor(x_me, d)
    visible = slack >= (x_me - asker) * tok
    factor = HD**-0.5 * LOG2E
    q_parts = []
    for b in range(blocks):
        q_rows = q_ref[b * tok : (b + 1) * tok, :]
        q_parts += [q_rows[:, h * HD : (h + 1) * HD] for h in range(SHARE)]
    q_rows = jnp.concatenate(q_parts, axis=0)
    q_rows = jnp.concatenate([q_rows, jnp.zeros((blocks * rows, HD), BF16)], axis=1)
    pairs = []
    scores = {}
    for kb in range(blocks):
        pair = k_ref[:, kb * tok : (kb + 1) * tok, :].reshape(span, 2 * HD)
        s = lax.dot_general(
            q_rows[kb * rows :], pair, (((1,), (1,)), ((), ())), preferred_element_type=F32
        )
        pairs.append(pair)
        for b in range(kb, blocks):
            part = s[(b - kb) * rows : (b - kb + 1) * rows]
            scores[b, kb] = jnp.where(visible, part, NEG) if b == kb else part
    peaks = []
    for b in range(blocks):
        peak = functools.reduce(jnp.maximum, [scores[b, kb] for kb in range(b + 1)])
        peaks.append(jnp.max(peak, axis=-1, keepdims=True) * factor)
    totals = [jnp.zeros((rows, span), F32) for _ in range(blocks)]
    sums = [jnp.zeros((rows, 2 * HD), F32) for _ in range(blocks)]
    for kb in range(blocks):
        probs = []
        for b in range(kb, blocks):
            p = jnp.exp2(scores[b, kb] * factor - peaks[b])
            totals[b] += p
            probs.append(p.astype(BF16))
        got = jnp.dot(jnp.concatenate(probs, axis=0), pairs[kb], preferred_element_type=F32)
        for b in range(kb, blocks):
            sums[b] += got[(b - kb) * rows : (b - kb + 1) * rows]
    lane = lax.broadcasted_iota(jnp.int32, (tok, 2 * HD), 1)
    for b in range(blocks):
        total = jnp.sum(totals[b], axis=-1, keepdims=True)
        result = (sums[b][:, HD:] / total).astype(BF16)
        weight = peaks[b] + jnp.log(total) * LOG2E
        high = weight.astype(BF16).astype(F32)
        low = weight - high
        notes = jnp.zeros((tok, 2 * HD), F32)
        for h in range(SHARE):
            part = slice(h * tok, (h + 1) * tok)
            notes = jnp.where(lane == h, high[part], notes)
            notes = jnp.where(lane == SHARE + h, low[part], notes)
        o_ref[b * tok : (b + 1) * tok, :] = jnp.concatenate(
            [result[h * tok : (h + 1) * tok] for h in range(SHARE)] + [notes.astype(BF16)], axis=1
        )


def combine_kernel(scal, o0, o1, o2, o3, a_ref):
    parts = [o0[...], o1[...], o2[...], o3[...]]
    notes = [part[:, QW:].astype(F32) for part in parts]
    for h in range(SHARE):
        weights = [n[:, h : h + 1] + n[:, SHARE + h : SHARE + h + 1] for n in notes]
        peak = functools.reduce(jnp.maximum, weights)
        weights = [jnp.exp2(w - peak) for w in weights]
        total = functools.reduce(jnp.add, weights)
        cols = slice(h * HD, (h + 1) * HD)
        mixed = functools.reduce(
            jnp.add, [w / total * part[:, cols].astype(F32) for w, part in zip(weights, parts)]
        )
        a_ref[:, cols] = mixed.astype(BF16)


def output(me, piece_refs, h_ref, w_of, o_ref):
    total = h_ref[...].astype(F32)
    update = jnp.zeros(total.shape, F32)
    for mask, value in in_order(piece_refs):
        update += jnp.dot(value, w_of(jnp.bitwise_xor(me, mask)), preferred_element_type=F32)
    o_ref[...] = (total + update).astype(BF16)


def output_kernel(scal, a0, a1, a2, a3, a4, h_ref, w_ref, o_ref):
    def w_of(owner):
        return w_ref[pl.ds(XN * owner, XN), 0].reshape(QW, QW)

    output(scal[0], [a0, a1, a2, a3, a4], h_ref, w_of, o_ref)


def first_output_kernel(scal, a0, a1, a2, a3, a4, h_ref, w0, w1, w2, w3, o_ref, held):
    assemble(scal[1], [w0, w1, w2, w3], held)
    output(scal[0], [a0, a1, a2, a3, a4], h_ref, lambda owner: held[:, owner].reshape(QW, QW), o_ref)


def whole(shape):
    return pl.BlockSpec(shape, lambda i, scal: (0,) * len(shape))


def in_place():
    return pl.BlockSpec(memory_space=pl.ANY)


def call(kernel, scal, args, in_specs, out_shape, flops, bytes_accessed, exps=0, scratch=(), own=None):
    outs = out_shape if isinstance(out_shape, list) else [out_shape]
    out_specs = [whole(o.shape) for o in outs]
    aliases = {}
    if own is not None:
        out_specs[own[1]] = in_place()
        aliases = {own[0] + 1: own[1]}
    single = not isinstance(out_shape, list)
    return pl.pallas_call(
        kernel,
        out_shape=out_shape,
        grid_spec=pltpu.PrefetchScalarGridSpec(
            num_scalar_prefetch=1,
            grid=(1,),
            in_specs=in_specs,
            out_specs=out_specs[0] if single else out_specs,
            scratch_shapes=list(scratch),
        ),
        input_output_aliases=aliases,
        compiler_params=pltpu.CompilerParams(vmem_limit_bytes=48 * 1024 * 1024),
        cost_estimate=pl.CostEstimate(flops=flops, bytes_accessed=bytes_accessed, transcendentals=exps),
    )(scal, *args)


def local(inputs, norm_gain, w_query, w_key, w_value, w_out):
    blocks, tok, width = inputs.shape
    rows = blocks * tok
    me = lax.axis_index("section")
    seq = lax.axis_index("seq")
    layers = lax.axis_size("section")
    shard = w_query.shape[1]
    qkv_w = QW + 2 * HD
    all_w = QW + qkv_w

    def cut(w):
        return w[0].reshape(shard, SN, -1).transpose(1, 0, 2)

    gain_rows = jnp.pad(norm_gain.reshape(4, width // 4), ((0, 12), (0, all_w - width // 4)))
    mine = jnp.concatenate([cut(w_query), cut(w_out), cut(w_key), cut(w_value)], axis=-1)
    mine = jnp.concatenate([mine, jnp.broadcast_to(gain_rows[None], (SN, 16, all_w))], axis=1)
    by_layer = lax.all_to_all(mine, "section", split_axis=0, concat_axis=0, tiled=True)
    gains = by_layer[:, shard : shard + 4, : width // 4].reshape(layers, SN, 1, QW)

    with jax.named_scope("weights"):
        early = lax.all_gather(by_layer[1:4, :shard], "seq", axis=0)
        late = lax.all_gather(by_layer[4:, :shard], "seq", axis=0)
        first = jnp.broadcast_to(by_layer[None, 0, :shard], (ZN, shard, all_w))
        first = lax.all_to_all(
            first, "seq", split_axis=0, concat_axis=0, tiled=True, axis_index_groups=along_z()
        )
        first_qkv = jnp.concatenate([first[:, :, :QW], first[:, :, 2 * QW :]], axis=-1)
        first_out = first[:, :, QW : 2 * QW]
        first_qkv = [first_qkv] + [lax.ppermute(first_qkv, "seq", seq_pairs(d)) for d in (1, 2, 3)]
        first_out = [first_out] + [lax.ppermute(first_out, "seq", seq_pairs(d)) for d in (1, 2, 3)]

    flat = inputs.reshape(rows, width)

    def input_piece(mask):
        return lax.dynamic_slice_in_dim(flat, jnp.bitwise_xor(me, mask) * QW, QW, 1)

    pieces = [input_piece(2 * d) for d in range(4)]
    pieces.append(jnp.stack([input_piece(2 * d + 1) for d in range(4)]))

    piece_shape = jax.ShapeDtypeStruct((rows, QW), BF16)
    piece_specs = [whole((rows, QW))] * 4 + [whole((4, rows, QW))]
    kv_shape = jax.ShapeDtypeStruct((ZN, rows, 2 * HD), BF16)
    part_shape = jax.ShapeDtypeStruct((rows, QW + 2 * HD), BF16)
    out_shape = jax.ShapeDtypeStruct((rows, width), BF16)
    gain_spec = pl.BlockSpec((1, SN, 1, QW), lambda i, scal: (scal[3], 0, 0, 0))
    sems = [pltpu.SemaphoreType.DMA((SN,))]
    seq_keys = ZN * XN * tok
    project_cost = (2 * rows * width * qkv_w, 2 * (width * qkv_w + rows * width))
    output_cost = (2 * rows * width * QW, 2 * (width * QW + rows * width))

    def weight_spec(width_, index):
        return pl.BlockSpec((ZN * XN, 1, shard, width_), lambda i, scal: (0, scal[2], 0, index))

    def exchange(q, kv):
        with jax.named_scope("exchange"):
            qs = [q] + [lax.ppermute(q, "seq", seq_pairs(d)) for d in (1, 2, 3)]
            kv = lax.all_to_all(
                kv, "seq", split_axis=0, concat_axis=0, tiled=True, axis_index_groups=along_z()
            )
        return qs, kv

    def attend(scal, qs, kv):
        parts = [None] * XN
        with jax.named_scope("attend"):
            for d in (2, 1, 3, 0):
                part = call(
                    functools.partial(attend_kernel, d=d, blocks=blocks, tok=tok),
                    scal,
                    (qs[d], kv),
                    [whole((rows, QW)), whole(kv_shape.shape)],
                    part_shape,
                    SHARE * tok * seq_keys * 128 * 6,
                    2 * (ZN * rows * 128 + 3 * rows * QW),
                    SHARE * tok * seq_keys * 6 // 4,
                )
                parts[d] = lax.ppermute(part, "seq", seq_pairs(d)) if d else part
            attended = call(
                combine_kernel,
                scal,
                parts,
                [whole(part_shape.shape)] * XN,
                piece_shape,
                10 * rows * QW,
                10 * rows * QW,
            )
            return spread(attended)

    def numbers(slot, layer):
        return jnp.stack([jnp.asarray(v, jnp.int32) for v in (me, seq, slot, layer)])

    scal = numbers(0, 0)
    with jax.named_scope("project"):
        q, kv = call(
            first_project_kernel,
            scal,
            (gains, *pieces, *first_qkv),
            [gain_spec] + piece_specs + [whole((ZN, shard, qkv_w))] * XN,
            [piece_shape, kv_shape],
            *project_cost,
            scratch=[pltpu.VMEM((XN, ZN, shard, qkv_w), BF16)],
        )
    qs, kv = exchange(q, kv)
    kv, first_out = lax.optimization_barrier((kv, first_out))
    heads = attend(scal, qs, kv)
    with jax.named_scope("output"):
        own = call(
            first_output_kernel,
            scal,
            (*heads, pieces[0], *first_out),
            piece_specs + [whole((rows, QW))] + [whole((ZN, shard, QW))] * XN,
            piece_shape,
            *output_cost,
            scratch=[pltpu.VMEM((XN, ZN, shard, QW), BF16)],
        )
        pieces = spread(own)
    out = jnp.zeros((rows, width), BF16)

    def step(group, first_layer):
        def body(layer, carry):
            pieces, out = carry
            scal = numbers(layer - first_layer, layer)
            with jax.named_scope("project"):
                q, kv, out = call(
                    project_kernel,
                    scal,
                    (gains, *pieces, group, group, out),
                    [gain_spec] + piece_specs + [weight_spec(QW, 0), weight_spec(2 * HD, 4), in_place()],
                    [piece_shape, kv_shape, out_shape],
                    *project_cost,
                    scratch=sems,
                    own=(8, 2),
                )
            heads = attend(scal, *exchange(q, kv))
            with jax.named_scope("output"):
                own = call(
                    output_kernel,
                    scal,
                    (*heads, pieces[0], group),
                    piece_specs + [whole((rows, QW)), weight_spec(QW, 1)],
                    piece_shape,
                    *output_cost,
                )
                return spread(own), out

        return body

    carry = (pieces, out)
    for group, begin, end in ((early, 1, 4), (late, 4, layers)):
        if LOOPED:
            carry = lax.fori_loop(begin, end, step(group, begin), carry)
        else:
            for layer in range(begin, end):
                carry = step(group, begin)(layer, carry)
    pieces, out = carry
    out = call(
        place_kernel,
        numbers(0, layers),
        (*pieces, out),
        piece_specs + [in_place()],
        out_shape,
        0,
        4 * rows * width,
        scratch=sems,
        own=(5, 0),
    )
    return out.reshape(1, blocks, tok, width)


def solution(mesh):
    in_specs = (
        P(None, "seq", None),
        P("section", None),
        P("section", "seq", None),
        P("section", "seq", None),
        P("section", "seq", None),
        P("section", "seq", None),
    )
    out_specs = P("section", None, "seq", None)
    return jax.shard_map(local, mesh=mesh, in_specs=in_specs, out_specs=out_specs, check_vma=False)
```

```python
import functools

import jax
import jax.numpy as jnp
from jax import lax
from jax.experimental import pallas as pl
from jax.experimental.pallas import tpu as pltpu
from jax.sharding import PartitionSpec as P

HEADS = 32
KVH = 8
HD = 64
SHARE = HEADS // KVH
QW = SHARE * HD
EPS = 1e-05
NEG = -1e30
LOG2E = 1.4426950408889634
LOOPED = True

ZN = 8
XN = 4
SN = 8
F32 = jnp.float32
BF16 = jnp.bfloat16


def seq_pairs(mask):
    return [(i, i ^ mask) for i in range(ZN * XN)]


def section_pairs(mask):
    return [(i, i ^ mask) for i in range(SN)]


def along_z():
    return [[z * XN + x for z in range(ZN)] for x in range(XN)]


def spread(piece):
    near = [piece] + [lax.ppermute(piece, "section", section_pairs(2 * d)) for d in (1, 2, 3)]
    other = lax.ppermute(jnp.stack(near), "section", section_pairs(1))
    return near + [other]


def in_order(refs):
    out = [(2 * d, refs[d][...]) for d in range(4)]
    out += [(2 * d + 1, refs[4][d]) for d in range(4)]
    return out


def place(me, layer, piece_refs, out_ref, sems):
    def copies():
        for i, (mask, source) in enumerate(sources(piece_refs)):
            first = pl.multiple_of(jnp.bitwise_xor(me, mask) * QW, QW)
            yield pltpu.make_async_copy(source, out_ref.at[:, pl.ds(first, QW)], sems.at[i])

    @pl.when(me == layer - 1)
    def _():
        for copy in copies():
            copy.start()
        for copy in copies():
            copy.wait()


def sources(refs):
    out = [(2 * d, refs[d]) for d in range(4)]
    return out + [(2 * d + 1, refs[4].at[d]) for d in range(4)]


def place_kernel(scal, p0, p1, p2, p3, p4, out_in, out_ref, sems):
    place(scal[0], scal[3], [p0, p1, p2, p3, p4], out_ref, sems)


ORDER = (0, 2, 4, 6, 1, 3, 5, 7)


def stream(me, slot, w_ref, first, held, sems):
    copies = []
    for i, mask in enumerate(ORDER):
        owner = jnp.bitwise_xor(me, mask)
        source = w_ref.at[pl.ds(XN * owner, XN), slot, :, first : first + held.shape[-1]]
        copies.append(pltpu.make_async_copy(source, held.at[i], sems.at[i]))
    for copy in copies:
        copy.start()
    return copies


def streamed(copies, held):
    def w_of(i):
        copies[i].wait()
        return held[i].reshape(QW, held.shape[-1])

    return w_of


def assembled(me, seq, parts, held, first):
    x_me = jnp.bitwise_and(seq, XN - 1)
    width = held.shape[-1]
    for d in range(XN):
        held[jnp.bitwise_xor(x_me, d)] = parts[d][:, :, first : first + width]
    return lambda i: held[:, jnp.bitwise_xor(me, ORDER[i])].reshape(QW, width)


def project(me, gain_ref, piece_refs, w_of):
    pieces = [(mask, value.astype(F32)) for mask, value in in_order(piece_refs)]
    width = sum(value.shape[1] for _, value in pieces)
    squares = functools.reduce(jnp.add, [value * value for _, value in pieces])
    scale = lax.rsqrt(jnp.sum(squares, axis=-1, keepdims=True) / width + EPS)
    total = None
    for i, (mask, value) in enumerate(pieces):
        gain = gain_ref[0, pl.ds(jnp.bitwise_xor(me, mask), 1), 0, :].astype(F32)
        normed = (value * scale * gain).astype(BF16)
        part = jnp.dot(normed, w_of(i), preferred_element_type=F32)
        total = part if total is None else total + part
    return total.astype(BF16)


def write_keys(pair, kv_ref):
    for i in range(kv_ref.shape[0]):
        kv_ref[i] = pair


def keys_kernel(scal, gain_ref, p0, p1, p2, p3, p4, w_ref, kv_ref, held, sems):
    w_of = streamed(stream(scal[0], scal[2], w_ref, QW, held, sems), held)
    write_keys(project(scal[0], gain_ref, [p0, p1, p2, p3, p4], w_of), kv_ref)


def queries_kernel(
    scal, gain_ref, p0, p1, p2, p3, p4, w_ref, out_in, q_ref, out_ref, held, sems, out_sems
):
    refs = [p0, p1, p2, p3, p4]
    w_of = streamed(stream(scal[0], scal[2], w_ref, 0, held, sems), held)
    q_ref[...] = project(scal[0], gain_ref, refs, w_of)
    place(scal[0], scal[3], refs, out_ref, out_sems)


def first_keys_kernel(scal, gain_ref, p0, p1, p2, p3, p4, w0, w1, w2, w3, kv_ref, held):
    w_of = assembled(scal[0], scal[1], [w0, w1, w2, w3], held, QW)
    write_keys(project(scal[0], gain_ref, [p0, p1, p2, p3, p4], w_of), kv_ref)


def first_queries_kernel(scal, gain_ref, p0, p1, p2, p3, p4, w0, w1, w2, w3, q_ref, held):
    w_of = assembled(scal[0], scal[1], [w0, w1, w2, w3], held, 0)
    q_ref[...] = project(scal[0], gain_ref, [p0, p1, p2, p3, p4], w_of)


def attend_kernel(scal, q_ref, k_ref, o_ref, *, d, blocks, tok):
    seq = scal[1]
    x_me = jnp.bitwise_and(seq, XN - 1)
    span = ZN * tok
    rows = SHARE * tok
    row = lax.rem(lax.broadcasted_iota(jnp.int32, (rows, 1), 0), tok)
    col = lax.broadcasted_iota(jnp.int32, (1, span), 1)
    col = lax.div(col, tok) * (XN * tok) + lax.rem(col, tok)
    asker = seq - x_me + jnp.bitwise_xor(x_me, d)
    visible = col <= row + (asker - x_me) * tok
    factor = HD**-0.5 * LOG2E
    q_parts = []
    for b in range(blocks):
        q_rows = q_ref[b * tok : (b + 1) * tok, :]
        q_parts += [q_rows[:, h * HD : (h + 1) * HD] for h in range(SHARE)]
    q_rows = jnp.concatenate(q_parts, axis=0)
    q_rows = jnp.concatenate([q_rows, jnp.zeros((blocks * rows, HD), BF16)], axis=1)
    pairs = []
    scores = {}
    key_lane = lax.broadcasted_iota(jnp.int32, (span, 2 * HD), 1) < HD
    for kb in range(blocks):
        pair = k_ref[:, kb * tok : (kb + 1) * tok, :].reshape(span, 2 * HD)
        s = lax.dot_general(
            q_rows[kb * rows :], pair, (((1,), (1,)), ((), ())), preferred_element_type=F32
        )
        pairs.append(jnp.where(key_lane, jnp.ones_like(pair), pair))
        for b in range(kb, blocks):
            part = s[(b - kb) * rows : (b - kb + 1) * rows]
            scores[b, kb] = jnp.where(visible, part, NEG) if b == kb else part
    peaks = []
    for b in range(blocks):
        peak = functools.reduce(jnp.maximum, [scores[b, kb] for kb in range(b + 1)])
        peaks.append(jnp.max(peak, axis=-1, keepdims=True) * factor)
    sums = [jnp.zeros((rows, 2 * HD), F32) for _ in range(blocks)]
    for kb in range(blocks):
        probs = []
        for b in range(kb, blocks):
            p = jnp.exp2(scores[b, kb] * factor - peaks[b])
            probs.append(p.astype(BF16))
        got = jnp.dot(jnp.concatenate(probs, axis=0), pairs[kb], preferred_element_type=F32)
        for b in range(kb, blocks):
            sums[b] += got[(b - kb) * rows : (b - kb + 1) * rows]
    lane = lax.broadcasted_iota(jnp.int32, (tok, 2 * HD), 1)
    for b in range(blocks):
        total = sums[b][:, :1]
        result = (sums[b][:, HD:] / total).astype(BF16)
        weight = peaks[b] + jnp.log(total) * LOG2E
        high = weight.astype(BF16).astype(F32)
        low = weight - high
        notes = jnp.zeros((tok, 2 * HD), F32)
        for h in range(SHARE):
            part = slice(h * tok, (h + 1) * tok)
            notes = jnp.where(lane == h, high[part], notes)
            notes = jnp.where(lane == SHARE + h, low[part], notes)
        o_ref[b * tok : (b + 1) * tok, :] = jnp.concatenate(
            [result[h * tok : (h + 1) * tok] for h in range(SHARE)] + [notes.astype(BF16)], axis=1
        )


def combine_kernel(scal, o0, o1, o2, o3, a_ref):
    parts = [o0[...], o1[...], o2[...], o3[...]]
    notes = [part[:, QW:].astype(F32) for part in parts]
    for h in range(SHARE):
        weights = [n[:, h : h + 1] + n[:, SHARE + h : SHARE + h + 1] for n in notes]
        peak = functools.reduce(jnp.maximum, weights)
        weights = [jnp.exp2(w - peak) for w in weights]
        total = functools.reduce(jnp.add, weights)
        cols = slice(h * HD, (h + 1) * HD)
        mixed = functools.reduce(
            jnp.add, [w / total * part[:, cols].astype(F32) for w, part in zip(weights, parts)]
        )
        a_ref[:, cols] = mixed.astype(BF16)


def output(piece_refs, h_ref, w_of, o_ref):
    total = h_ref[...].astype(F32)
    update = jnp.zeros(total.shape, F32)
    for i, (_, value) in enumerate(in_order(piece_refs)):
        update += jnp.dot(value, w_of(i), preferred_element_type=F32)
    o_ref[...] = (total + update).astype(BF16)


def output_kernel(scal, a0, a1, a2, a3, a4, h_ref, w_ref, o_ref, held, sems):
    w_of = streamed(stream(scal[0], scal[2], w_ref, QW + 2 * HD, held, sems), held)
    output([a0, a1, a2, a3, a4], h_ref, w_of, o_ref)


def first_output_kernel(scal, a0, a1, a2, a3, a4, h_ref, w0, w1, w2, w3, o_ref, held):
    w_of = assembled(scal[0], scal[1], [w0, w1, w2, w3], held, 0)
    output([a0, a1, a2, a3, a4], h_ref, w_of, o_ref)


def whole(shape):
    return pl.BlockSpec(shape, lambda i, scal: (0,) * len(shape))


def in_place():
    return pl.BlockSpec(memory_space=pl.ANY)


def call(kernel, scal, args, in_specs, out_shape, flops, bytes_accessed, exps=0, scratch=(), own=None):
    outs = out_shape if isinstance(out_shape, list) else [out_shape]
    out_specs = [whole(o.shape) for o in outs]
    aliases = {}
    if own is not None:
        out_specs[own[1]] = in_place()
        aliases = {own[0] + 1: own[1]}
    single = not isinstance(out_shape, list)
    return pl.pallas_call(
        kernel,
        out_shape=out_shape,
        grid_spec=pltpu.PrefetchScalarGridSpec(
            num_scalar_prefetch=1,
            grid=(1,),
            in_specs=in_specs,
            out_specs=out_specs[0] if single else out_specs,
            scratch_shapes=list(scratch),
        ),
        input_output_aliases=aliases,
        compiler_params=pltpu.CompilerParams(vmem_limit_bytes=48 * 1024 * 1024),
        cost_estimate=pl.CostEstimate(flops=flops, bytes_accessed=bytes_accessed, transcendentals=exps),
    )(scal, *args)


def local(inputs, norm_gain, w_query, w_key, w_value, w_out):
    blocks, tok, width = inputs.shape
    rows = blocks * tok
    me = lax.axis_index("section")
    seq = lax.axis_index("seq")
    layers = lax.axis_size("section")
    shard = w_query.shape[1]
    qkv_w = QW + 2 * HD
    all_w = QW + qkv_w

    def cut(w):
        return w[0].reshape(shard, SN, -1).transpose(1, 0, 2)

    gain_rows = jnp.pad(norm_gain.reshape(4, width // 4), ((0, 12), (0, all_w - width // 4)))
    mine = jnp.concatenate([cut(w_query), cut(w_key), cut(w_value), cut(w_out)], axis=-1)
    mine = jnp.concatenate([mine, jnp.broadcast_to(gain_rows[None], (SN, 16, all_w))], axis=1)
    by_layer = lax.all_to_all(mine, "section", split_axis=0, concat_axis=0, tiled=True)
    gains = by_layer[:, shard : shard + 4, : width // 4].reshape(layers, SN, 1, QW)

    with jax.named_scope("weights"):
        early = lax.all_gather(by_layer[1:4, :shard], "seq", axis=0)
        late = lax.all_gather(by_layer[4:, :shard], "seq", axis=0)

        def over_z(part):
            part = jnp.broadcast_to(part[None], (ZN,) + part.shape)
            return lax.all_to_all(
                part, "seq", split_axis=0, concat_axis=0, tiled=True, axis_index_groups=along_z()
            )

        def over_x(part):
            return [part] + [lax.ppermute(part, "seq", seq_pairs(d)) for d in (1, 2, 3)]

        first_qkv = over_z(by_layer[0, :shard, :qkv_w])
        first_qkv, first_out = lax.optimization_barrier((first_qkv, by_layer[0, :shard, qkv_w:]))
        first_qkv, first_out = lax.optimization_barrier((over_x(first_qkv), over_z(first_out)))
        first_out = over_x(first_out)

    flat = inputs.reshape(rows, width)

    def input_piece(mask):
        return lax.dynamic_slice_in_dim(flat, jnp.bitwise_xor(me, mask) * QW, QW, 1)

    pieces = [input_piece(2 * d) for d in range(4)]
    pieces.append(jnp.stack([input_piece(2 * d + 1) for d in range(4)]))

    piece_shape = jax.ShapeDtypeStruct((rows, QW), BF16)
    piece_specs = [whole((rows, QW))] * 4 + [whole((4, rows, QW))]
    kv_shape = jax.ShapeDtypeStruct((ZN, rows, 2 * HD), BF16)
    part_shape = jax.ShapeDtypeStruct((rows, QW + 2 * HD), BF16)
    out_shape = jax.ShapeDtypeStruct((rows, width), BF16)
    gain_spec = pl.BlockSpec((1, SN, 1, QW), lambda i, scal: (scal[3], 0, 0, 0))
    sems = [pltpu.SemaphoreType.DMA((SN,))]
    seq_keys = ZN * XN * tok
    keys_cost = (4 * rows * width * HD, 2 * (width * 2 * HD + rows * width))
    full_cost = (2 * rows * width * QW, 2 * (width * QW + rows * width))

    def room(width_):
        return [pltpu.VMEM((SN, XN, shard, width_), BF16), pltpu.SemaphoreType.DMA((SN,))]

    def first_room(width_):
        return [pltpu.VMEM((XN, ZN, shard, width_), BF16)]

    def exchange(q, kv):
        with jax.named_scope("exchange"):
            qs = [q] + [lax.ppermute(q, "seq", seq_pairs(d)) for d in (1, 2, 3)]
            kv = lax.all_to_all(
                kv, "seq", split_axis=0, concat_axis=0, tiled=True, axis_index_groups=along_z()
            )
        return qs, kv

    def attend(scal, qs, kv):
        parts = [None] * XN
        with jax.named_scope("attend"):
            for d in (2, 1, 3, 0):
                part = call(
                    functools.partial(attend_kernel, d=d, blocks=blocks, tok=tok),
                    scal,
                    (qs[d], kv),
                    [whole((rows, QW)), whole(kv_shape.shape)],
                    part_shape,
                    SHARE * tok * seq_keys * 128 * 6,
                    2 * (ZN * rows * 128 + 3 * rows * QW),
                    SHARE * tok * seq_keys * 6 // 4,
                )
                parts[d] = lax.ppermute(part, "seq", seq_pairs(d)) if d else part
            attended = call(
                combine_kernel,
                scal,
                parts,
                [whole(part_shape.shape)] * XN,
                piece_shape,
                10 * rows * QW,
                10 * rows * QW,
            )
            return spread(attended)

    def numbers(slot, layer):
        return jnp.stack([jnp.asarray(v, jnp.int32) for v in (me, seq, slot, layer)])

    scal = numbers(0, 0)
    first_specs = [gain_spec] + piece_specs + [whole((ZN, shard, qkv_w))] * XN
    with jax.named_scope("project"):
        args = (gains, *pieces, *first_qkv)
        kv = call(first_keys_kernel, scal, args, first_specs, kv_shape, *keys_cost, scratch=first_room(2 * HD))
        q = call(first_queries_kernel, scal, args, first_specs, piece_shape, *full_cost, scratch=first_room(QW))
    qs, kv = exchange(q, kv)
    kv, first_out = lax.optimization_barrier((kv, first_out))
    heads = attend(scal, qs, kv)
    with jax.named_scope("output"):
        own = call(
            first_output_kernel,
            scal,
            (*heads, pieces[0], *first_out),
            piece_specs + [whole((rows, QW))] + [whole((ZN, shard, QW))] * XN,
            piece_shape,
            *full_cost,
            scratch=first_room(QW),
        )
        pieces = spread(own)
    out = jnp.zeros((rows, width), BF16)

    def step(group, first_layer):
        def body(layer, carry):
            pieces, out = carry
            scal = numbers(layer - first_layer, layer)
            with jax.named_scope("project"):
                specs = [gain_spec] + piece_specs + [in_place()]
                args = (gains, *pieces, group)
                kv = call(keys_kernel, scal, args, specs, kv_shape, *keys_cost, scratch=room(2 * HD))
                q, out = call(
                    queries_kernel,
                    scal,
                    (*args, out),
                    specs + [in_place()],
                    [piece_shape, out_shape],
                    *full_cost,
                    scratch=room(QW) + sems,
                    own=(7, 1),
                )
            heads = attend(scal, *exchange(q, kv))
            with jax.named_scope("output"):
                own = call(
                    output_kernel,
                    scal,
                    (*heads, pieces[0], group),
                    piece_specs + [whole((rows, QW)), in_place()],
                    piece_shape,
                    *full_cost,
                    scratch=room(QW),
                )
                return spread(own), out

        return body

    carry = (pieces, out)
    for group, begin, end in ((early, 1, 4), (late, 4, layers)):
        if LOOPED:
            carry = lax.fori_loop(begin, end, step(group, begin), carry)
        else:
            for layer in range(begin, end):
                carry = step(group, begin)(layer, carry)
    pieces, out = carry
    out = call(
        place_kernel,
        numbers(0, layers),
        (*pieces, out),
        piece_specs + [in_place()],
        out_shape,
        0,
        4 * rows * width,
        scratch=sems,
        own=(5, 0),
    )
    return out.reshape(1, blocks, tok, width)


def solution(mesh):
    in_specs = (
        P(None, "seq", None),
        P("section", None),
        P("section", "seq", None),
        P("section", "seq", None),
        P("section", "seq", None),
        P("section", "seq", None),
    )
    out_specs = P("section", None, "seq", None)
    return jax.shard_map(local, mesh=mesh, in_specs=in_specs, out_specs=out_specs, check_vma=False)
```

```python
import functools

import jax
import jax.numpy as jnp
from jax import lax
from jax.experimental import pallas as pl
from jax.experimental.pallas import tpu as pltpu
from jax.sharding import PartitionSpec as P

HEADS = 32
KVH = 8
HD = 64
SHARE = HEADS // KVH
QW = SHARE * HD
EPS = 1e-05
NEG = -1e30
LOG2E = 1.4426950408889634
SHARD = 64
Q_ROWS = QW // 128 * SHARD
QKV_ROWS = Q_ROWS + SHARD
ALL_ROWS = QKV_ROWS + Q_ROWS

ZN = 8
XN = 4
SN = 8
F32 = jnp.float32
BF16 = jnp.bfloat16


def seq_pairs(mask):
    return [(i, i ^ mask) for i in range(ZN * XN)]


def section_pairs(mask):
    return [(i, i ^ mask) for i in range(SN)]


def along_z():
    return [[z * XN + x for z in range(ZN)] for x in range(XN)]


def spread(piece):
    near = [piece] + [lax.ppermute(piece, "section", section_pairs(2 * d)) for d in (1, 2, 3)]
    other = lax.ppermute(jnp.stack(near), "section", section_pairs(1))
    return near + [other]


def in_order(refs):
    out = [(2 * d, refs[d][...]) for d in range(4)]
    out += [(2 * d + 1, refs[4][d]) for d in range(4)]
    return out


def place(me, layer, piece_refs, out_ref, sems):
    def copies():
        for i, (mask, source) in enumerate(sources(piece_refs)):
            first = pl.multiple_of(jnp.bitwise_xor(me, mask) * QW, QW)
            yield pltpu.make_async_copy(source, out_ref.at[:, pl.ds(first, QW)], sems.at[i])

    @pl.when(me == layer - 1)
    def _():
        for copy in copies():
            copy.start()
        for copy in copies():
            copy.wait()


def sources(refs):
    out = [(2 * d, refs[d]) for d in range(4)]
    return out + [(2 * d + 1, refs[4].at[d]) for d in range(4)]


def place_kernel(scal, p0, p1, p2, p3, p4, out_in, out_ref, sems):
    place(scal[0], scal[3], [p0, p1, p2, p3, p4], out_ref, sems)


ORDER = (0, 2, 4, 6, 1, 3, 5, 7)


def lanes(block):
    panels = block.shape[1] // SHARD
    parts = [block[:, p * SHARD : (p + 1) * SHARD, :].reshape(XN * SHARD, 128) for p in range(panels)]
    return parts[0] if panels == 1 else jnp.concatenate(parts, axis=1)


def stream(me, slot, w_ref, held, sems):
    copies = []
    for i, mask in enumerate(ORDER):
        owner = jnp.bitwise_xor(me, mask)
        source = w_ref.at[pl.ds(XN * owner, XN), slot, 0:Q_ROWS, :]
        copies.append(pltpu.make_async_copy(source, held.at[i], sems.at[i]))
    for copy in copies:
        copy.start()

    def w_of(i):
        copies[i].wait()
        return lanes(held[i])

    return w_of


def resident(me, w_ref):
    return lambda i: lanes(w_ref[pl.ds(XN * jnp.bitwise_xor(me, ORDER[i]), XN)])


def assembled(me, seq, parts, held, first):
    x_me = jnp.bitwise_and(seq, XN - 1)
    count = held.shape[2]
    for d in range(XN):
        held[jnp.bitwise_xor(x_me, d)] = parts[d][:, first : first + count, :]
    return lambda i: lanes(held[:, jnp.bitwise_xor(me, ORDER[i])])


def project(me, gain_ref, layer, piece_refs, w_of):
    pieces = [(mask, value.astype(F32)) for mask, value in in_order(piece_refs)]
    width = sum(value.shape[1] for _, value in pieces)
    squares = functools.reduce(jnp.add, [value * value for _, value in pieces])
    scale = lax.rsqrt(jnp.sum(squares, axis=-1, keepdims=True) / width + EPS)
    total = None
    for i, (mask, value) in enumerate(pieces):
        owner = jnp.bitwise_xor(me, mask)
        gain = gain_ref[layer, pl.ds(owner, 1), 0, :].astype(F32)
        normed = (value * scale * gain).astype(BF16)
        part = jnp.dot(normed, w_of(i), preferred_element_type=F32)
        total = part if total is None else total + part
    return total.astype(BF16)


def write_keys(pair, kv_ref):
    for i in range(kv_ref.shape[0]):
        kv_ref[i] = pair


def keys_kernel(scal, gain_ref, p0, p1, p2, p3, p4, wkv_ref, kv_ref):
    w_of = resident(scal[0], wkv_ref)
    write_keys(project(scal[0], gain_ref, scal[3], [p0, p1, p2, p3, p4], w_of), kv_ref)


def queries_kernel(
    scal, gain_ref, p0, p1, p2, p3, p4, w_ref, out_in, q_ref, out_ref, wout_ref, wkv_ref, held, sems, out_sems
):
    refs = [p0, p1, p2, p3, p4]
    slot = scal[2]
    w_of = stream(scal[0], slot, w_ref, held, sems)
    later = jnp.minimum(slot + 1, w_ref.shape[1] - 1)
    ahead = [
        pltpu.make_async_copy(w_ref.at[:, slot, QKV_ROWS:ALL_ROWS, :], wout_ref, sems.at[SN]),
        pltpu.make_async_copy(w_ref.at[:, later, Q_ROWS:QKV_ROWS, :], wkv_ref, sems.at[SN + 1]),
    ]
    for copy in ahead:
        copy.start()
    q_ref[...] = project(scal[0], gain_ref, scal[3], refs, w_of)
    place(scal[0], scal[3], refs, out_ref, out_sems)
    for copy in ahead:
        copy.wait()


def first_keys_kernel(scal, gain_ref, p0, p1, p2, p3, p4, w0, w1, w2, w3, kv_ref, held):
    w_of = assembled(scal[0], scal[1], [w0, w1, w2, w3], held, Q_ROWS)
    write_keys(project(scal[0], gain_ref, scal[3], [p0, p1, p2, p3, p4], w_of), kv_ref)


def first_queries_kernel(scal, gain_ref, p0, p1, p2, p3, p4, w0, w1, w2, w3, q_ref, held):
    w_of = assembled(scal[0], scal[1], [w0, w1, w2, w3], held, 0)
    q_ref[...] = project(scal[0], gain_ref, scal[3], [p0, p1, p2, p3, p4], w_of)


def attend_kernel(scal, q_ref, k_ref, o_ref, *, d, blocks, tok):
    seq = scal[1]
    x_me = jnp.bitwise_and(seq, XN - 1)
    span = ZN * tok
    rows = SHARE * tok
    row = lax.rem(lax.broadcasted_iota(jnp.int32, (rows, 1), 0), tok)
    col = lax.broadcasted_iota(jnp.int32, (1, span), 1)
    col = lax.div(col, tok) * (XN * tok) + lax.rem(col, tok)
    asker = seq - x_me + jnp.bitwise_xor(x_me, d)
    visible = col <= row + (asker - x_me) * tok
    factor = HD**-0.5 * LOG2E
    q_parts = []
    for b in range(blocks):
        q_rows = q_ref[b * tok : (b + 1) * tok, :]
        q_parts += [q_rows[:, h * HD : (h + 1) * HD] for h in range(SHARE)]
    q_rows = jnp.concatenate(q_parts, axis=0)
    q_rows = jnp.concatenate([q_rows, jnp.zeros((blocks * rows, HD), BF16)], axis=1)
    pairs = []
    scores = {}
    for kb in range(blocks):
        pair = k_ref[:, kb * tok : (kb + 1) * tok, :].reshape(span, 2 * HD)
        s = lax.dot_general(
            q_rows[kb * rows :], pair, (((1,), (1,)), ((), ())), preferred_element_type=F32
        )
        pairs.append(pair)
        for b in range(kb, blocks):
            part = s[(b - kb) * rows : (b - kb + 1) * rows]
            scores[b, kb] = jnp.where(visible, part, NEG) if b == kb else part
    peaks = []
    for b in range(blocks):
        peak = functools.reduce(jnp.maximum, [scores[b, kb] for kb in range(b + 1)])
        peaks.append(jnp.max(peak, axis=-1, keepdims=True) * factor)
    totals = [jnp.zeros((rows, span), F32) for _ in range(blocks)]
    sums = [jnp.zeros((rows, 2 * HD), F32) for _ in range(blocks)]
    for kb in range(blocks):
        probs = []
        for b in range(kb, blocks):
            p = jnp.exp2(scores[b, kb] * factor - peaks[b])
            totals[b] += p
            probs.append(p.astype(BF16))
        got = jnp.dot(jnp.concatenate(probs, axis=0), pairs[kb], preferred_element_type=F32)
        for b in range(kb, blocks):
            sums[b] += got[(b - kb) * rows : (b - kb + 1) * rows]
    lane = lax.broadcasted_iota(jnp.int32, (tok, 2 * HD), 1)
    for b in range(blocks):
        total = jnp.sum(totals[b], axis=-1, keepdims=True)
        result = (sums[b][:, HD:] / total).astype(BF16)
        weight = peaks[b] + jnp.log(total) * LOG2E
        high = weight.astype(BF16).astype(F32)
        low = weight - high
        notes = jnp.zeros((tok, 2 * HD), F32)
        for h in range(SHARE):
            part = slice(h * tok, (h + 1) * tok)
            notes = jnp.where(lane == h, high[part], notes)
            notes = jnp.where(lane == SHARE + h, low[part], notes)
        o_ref[b * tok : (b + 1) * tok, :] = jnp.concatenate(
            [result[h * tok : (h + 1) * tok] for h in range(SHARE)] + [notes.astype(BF16)], axis=1
        )


def combine_kernel(scal, o0, o1, o2, o3, a_ref):
    parts = [o0[...], o1[...], o2[...], o3[...]]
    notes = [part[:, QW:].astype(F32) for part in parts]
    for h in range(SHARE):
        weights = [n[:, h : h + 1] + n[:, SHARE + h : SHARE + h + 1] for n in notes]
        peak = functools.reduce(jnp.maximum, weights)
        weights = [jnp.exp2(w - peak) for w in weights]
        total = functools.reduce(jnp.add, weights)
        cols = slice(h * HD, (h + 1) * HD)
        mixed = functools.reduce(
            jnp.add, [w / total * part[:, cols].astype(F32) for w, part in zip(weights, parts)]
        )
        a_ref[:, cols] = mixed.astype(BF16)


def output(piece_refs, h_ref, w_of, o_ref):
    total = h_ref[...].astype(F32)
    update = jnp.zeros(total.shape, F32)
    for i, (_, value) in enumerate(in_order(piece_refs)):
        update += jnp.dot(value, w_of(i), preferred_element_type=F32)
    o_ref[...] = (total + update).astype(BF16)


def output_kernel(scal, a0, a1, a2, a3, a4, h_ref, wout_ref, o_ref):
    output([a0, a1, a2, a3, a4], h_ref, resident(scal[0], wout_ref), o_ref)


def first_output_kernel(scal, a0, a1, a2, a3, a4, h_ref, w0, w1, w2, w3, o_ref, held):
    w_of = assembled(scal[0], scal[1], [w0, w1, w2, w3], held, 0)
    output([a0, a1, a2, a3, a4], h_ref, w_of, o_ref)


VMEM = pl.BlockSpec(memory_space=pltpu.VMEM)
SMEM = pl.BlockSpec(memory_space=pltpu.SMEM)
ANY = pl.BlockSpec(memory_space=pl.ANY)


def call(kernel, scal, args, out_shape, flops, bytes_accessed, exps=0, scratch=(), big=(), own=None):
    outs = out_shape if isinstance(out_shape, list) else [out_shape]
    in_specs = [SMEM] + [ANY if i in big else VMEM for i in range(len(args))]
    out_specs = [VMEM] * len(outs)
    aliases = {}
    if own is not None:
        out_specs[own[1]] = ANY
        aliases = {own[0] + 1: own[1]}
    single = not isinstance(out_shape, list)
    return pl.pallas_call(
        kernel,
        out_shape=out_shape,
        in_specs=in_specs,
        out_specs=out_specs[0] if single else out_specs,
        scratch_shapes=list(scratch),
        input_output_aliases=aliases,
        compiler_params=pltpu.CompilerParams(vmem_limit_bytes=24 * 1024 * 1024),
        cost_estimate=pl.CostEstimate(flops=flops, bytes_accessed=bytes_accessed, transcendentals=exps),
    )(scal, *args)


def local(inputs, norm_gain, w_query, w_key, w_value, w_out):
    blocks, tok, width = inputs.shape
    rows = blocks * tok
    me = lax.axis_index("section")
    seq = lax.axis_index("seq")
    layers = lax.axis_size("section")
    shard = w_query.shape[1]
    assert shard == SHARD

    def panels(w):
        w = w.reshape(shard, SN, -1, 128)
        return w.transpose(1, 2, 0, 3).reshape(SN, -1, 128)

    pair = jnp.concatenate([w_key[0].reshape(shard, SN, HD), w_value[0].reshape(shard, SN, HD)], axis=-1)
    gain_rows = jnp.broadcast_to(norm_gain.reshape(1, width // 128, 128), (SN, width // 128, 128))
    mine = jnp.concatenate([panels(w_query[0]), panels(pair), panels(w_out[0]), gain_rows], axis=1)
    by_layer = lax.all_to_all(mine, "section", split_axis=0, concat_axis=0, tiled=True)
    gains = by_layer[:, ALL_ROWS:].reshape(layers, SN, 1, QW)
    by_layer = by_layer[:, :ALL_ROWS]

    with jax.named_scope("weights"):
        early = lax.all_gather(by_layer[1:4], "seq", axis=0)
        late = lax.all_gather(by_layer[4:], "seq", axis=0)

        def over_z(part):
            part = jnp.broadcast_to(part[None], (ZN,) + part.shape)
            return lax.all_to_all(
                part, "seq", split_axis=0, concat_axis=0, tiled=True, axis_index_groups=along_z()
            )

        def over_x(part):
            return [part] + [lax.ppermute(part, "seq", seq_pairs(d)) for d in (1, 2, 3)]

        first_qkv = over_z(by_layer[0, :QKV_ROWS])
        first_qkv, first_out = lax.optimization_barrier((first_qkv, by_layer[0, QKV_ROWS:]))
        first_qkv, first_out = lax.optimization_barrier((over_x(first_qkv), over_z(first_out)))
        first_out = over_x(first_out)

    flat = inputs.reshape(rows, width)

    def input_piece(mask):
        return lax.dynamic_slice_in_dim(flat, jnp.bitwise_xor(me, mask) * QW, QW, 1)

    pieces = [input_piece(2 * d) for d in range(4)]
    pieces.append(jnp.stack([input_piece(2 * d + 1) for d in range(4)]))

    piece_shape = jax.ShapeDtypeStruct((rows, QW), BF16)
    kv_shape = jax.ShapeDtypeStruct((ZN, rows, 2 * HD), BF16)
    part_shape = jax.ShapeDtypeStruct((rows, QW + 2 * HD), BF16)
    out_shape = jax.ShapeDtypeStruct((rows, width), BF16)
    seq_keys = ZN * XN * tok
    keys_cost = (4 * rows * width * HD, 2 * (width * 2 * HD + rows * width))
    full_cost = (2 * rows * width * QW, 2 * (width * QW + rows * width))

    def first_room(count):
        return [pltpu.VMEM((XN, ZN, count, 128), BF16)]

    def exchange(q, kv):
        with jax.named_scope("exchange"):
            qs = [q] + [lax.ppermute(q, "seq", seq_pairs(d)) for d in (1, 2, 3)]
            kv = lax.all_to_all(
                kv, "seq", split_axis=0, concat_axis=0, tiled=True, axis_index_groups=along_z()
            )
        return qs, kv

    def attend(scal, qs, kv):
        parts = [None] * XN
        with jax.named_scope("attend"):
            for d in (2, 1, 3, 0):
                part = call(
                    functools.partial(attend_kernel, d=d, blocks=blocks, tok=tok),
                    scal,
                    (qs[d], kv),
                    part_shape,
                    SHARE * tok * seq_keys * 128 * 6,
                    2 * (ZN * rows * 128 + 3 * rows * QW),
                    SHARE * tok * seq_keys * 6 // 4,
                )
                parts[d] = lax.ppermute(part, "seq", seq_pairs(d)) if d else part
            attended = call(
                combine_kernel,
                scal,
                parts,
                piece_shape,
                10 * rows * QW,
                10 * rows * QW,
            )
            return spread(attended)

    def numbers(slot, layer):
        return jnp.stack([jnp.asarray(v, jnp.int32) for v in (me, seq, slot, layer)])

    scal = numbers(0, 0)
    with jax.named_scope("project"):
        args = (gains, *pieces, *first_qkv)
        kv = call(first_keys_kernel, scal, args, kv_shape, *keys_cost, scratch=first_room(SHARD))
        q = call(first_queries_kernel, scal, args, piece_shape, *full_cost, scratch=first_room(Q_ROWS))
    qs, kv = exchange(q, kv)
    kv, first_out = lax.optimization_barrier((kv, first_out))
    heads = attend(scal, qs, kv)
    with jax.named_scope("output"):
        args = (*heads, pieces[0], *first_out)
        own = call(first_output_kernel, scal, args, piece_shape, *full_cost, scratch=first_room(Q_ROWS))
        pieces = spread(own)
    out = jnp.zeros((rows, width), BF16)

    wkv_shape = jax.ShapeDtypeStruct((ZN * XN, SHARD, 128), BF16)
    wout_shape = jax.ShapeDtypeStruct((ZN * XN, Q_ROWS, 128), BF16)
    query_room = [
        pltpu.VMEM((SN, XN, Q_ROWS, 128), BF16),
        pltpu.SemaphoreType.DMA((SN + 2,)),
        pltpu.SemaphoreType.DMA((SN,)),
    ]

    def step(group, first_layer):
        def body(layer, carry):
            pieces, out, wkv = carry
            scal = numbers(layer - first_layer, layer)
            with jax.named_scope("project"):
                kv = call(keys_kernel, scal, (gains, *pieces, wkv), kv_shape, *keys_cost)
                q, out, wout, wkv = call(
                    queries_kernel,
                    scal,
                    (gains, *pieces, group, out),
                    [piece_shape, out_shape, wout_shape, wkv_shape],
                    *full_cost,
                    scratch=query_room,
                    big=(6, 7),
                    own=(7, 1),
                )
            heads = attend(scal, *exchange(q, kv))
            with jax.named_scope("output"):
                own = call(output_kernel, scal, (*heads, pieces[0], wout), piece_shape, *full_cost)
                return spread(own), out, wkv

        return body

    for group, begin, end in ((early, 1, 4), (late, 4, layers)):
        carry = (pieces, out, group[:, 0, Q_ROWS:QKV_ROWS])
        pieces, out, _ = lax.fori_loop(begin, end, step(group, begin), carry)
    out = call(
        place_kernel,
        numbers(0, layers),
        (*pieces, out),
        out_shape,
        0,
        4 * rows * width,
        scratch=[pltpu.SemaphoreType.DMA((SN,))],
        big=(5,),
        own=(5, 0),
    )
    return out.reshape(1, blocks, tok, width)


def solution(mesh):
    in_specs = (
        P(None, "seq", None),
        P("section", None),
        P("section", "seq", None),
        P("section", "seq", None),
        P("section", "seq", None),
        P("section", "seq", None),
    )
    out_specs = P("section", None, "seq", None)
    return jax.shard_map(local, mesh=mesh, in_specs=in_specs, out_specs=out_specs, check_vma=False)
```

```python
import functools

import jax
import jax.numpy as jnp
from jax import lax
from jax.experimental import pallas as pl
from jax.experimental.pallas import tpu as pltpu
from jax.sharding import PartitionSpec as P

HEADS = 32
KVH = 8
HD = 64
SHARE = HEADS // KVH
QW = SHARE * HD
EPS = 1e-05
NEG = -1e30
LOG2E = 1.4426950408889634
SHARD = 64
Q_ROWS = QW // 128 * SHARD
QKV_ROWS = Q_ROWS + SHARD
ALL_ROWS = QKV_ROWS + Q_ROWS

ZN = 8
XN = 4
SN = 8
F32 = jnp.float32
BF16 = jnp.bfloat16


def seq_pairs(mask):
    return [(i, i ^ mask) for i in range(ZN * XN)]


def section_pairs(mask):
    return [(i, i ^ mask) for i in range(SN)]


def along_z():
    return [[z * XN + x for z in range(ZN)] for x in range(XN)]


def spread(piece):
    near = [piece] + [lax.ppermute(piece, "section", section_pairs(2 * d)) for d in (1, 2, 3)]
    other = lax.ppermute(jnp.stack(near), "section", section_pairs(1))
    return near + [other]


def in_order(refs):
    out = [(2 * d, refs[d][...]) for d in range(4)]
    out += [(2 * d + 1, refs[4][d]) for d in range(4)]
    return out


def place(me, layer, piece_refs, out_ref, sems):
    def copies():
        for i, (mask, source) in enumerate(sources(piece_refs)):
            first = pl.multiple_of(jnp.bitwise_xor(me, mask) * QW, QW)
            yield pltpu.make_async_copy(source, out_ref.at[:, pl.ds(first, QW)], sems.at[i])

    @pl.when(me == layer - 1)
    def _():
        for copy in copies():
            copy.start()
        for copy in copies():
            copy.wait()


def sources(refs):
    out = [(2 * d, refs[d]) for d in range(4)]
    return out + [(2 * d + 1, refs[4].at[d]) for d in range(4)]


def place_kernel(scal, p0, p1, p2, p3, p4, out_in, out_ref, sems):
    place(scal[0], scal[3], [p0, p1, p2, p3, p4], out_ref, sems)


ORDER = (0, 2, 4, 6, 1, 3, 5, 7)


def lanes(block):
    panels = block.shape[1] // SHARD
    parts = [block[:, p * SHARD : (p + 1) * SHARD, :].reshape(XN * SHARD, 128) for p in range(panels)]
    return parts[0] if panels == 1 else jnp.concatenate(parts, axis=1)


def stream(me, slot, w_ref, held, sems):
    copies = []
    for i, mask in enumerate(ORDER):
        owner = jnp.bitwise_xor(me, mask)
        source = w_ref.at[pl.ds(XN * owner, XN), slot, 0:Q_ROWS, :]
        copies.append(pltpu.make_async_copy(source, held.at[i], sems.at[i]))
    for copy in copies:
        copy.start()

    def w_of(i):
        copies[i].wait()
        return lanes(held[i])

    return w_of


def resident(me, w_ref):
    return lambda i: lanes(w_ref[pl.ds(XN * jnp.bitwise_xor(me, ORDER[i]), XN)])


def assembled(me, seq, parts, held, first):
    x_me = jnp.bitwise_and(seq, XN - 1)
    count = held.shape[2]
    for d in range(XN):
        held[jnp.bitwise_xor(x_me, d)] = parts[d][:, first : first + count, :]
    return lambda i: lanes(held[:, jnp.bitwise_xor(me, ORDER[i])])


def project(me, gain_ref, layer, piece_refs, w_of):
    pieces = [(mask, value.astype(F32)) for mask, value in in_order(piece_refs)]
    width = sum(value.shape[1] for _, value in pieces)
    squares = functools.reduce(jnp.add, [value * value for _, value in pieces])
    scale = lax.rsqrt(jnp.sum(squares, axis=-1, keepdims=True) / width + EPS)
    total = None
    for i, (mask, value) in enumerate(pieces):
        owner = jnp.bitwise_xor(me, mask)
        gain = gain_ref[layer, pl.ds(owner, 1), 0, :].astype(F32)
        normed = (value * scale * gain).astype(BF16)
        part = jnp.dot(normed, w_of(i), preferred_element_type=F32)
        total = part if total is None else total + part
    return total.astype(BF16)


def write_keys(pair, kv_ref):
    for i in range(kv_ref.shape[0]):
        kv_ref[i] = pair


def keys_kernel(scal, gain_ref, p0, p1, p2, p3, p4, wkv_ref, kv_ref):
    w_of = resident(scal[0], wkv_ref)
    write_keys(project(scal[0], gain_ref, scal[3], [p0, p1, p2, p3, p4], w_of), kv_ref)


def queries_kernel(
    scal, gain_ref, p0, p1, p2, p3, p4, w_ref, out_in, q_ref, out_ref, wout_ref, wkv_ref, held, sems, out_sems
):
    refs = [p0, p1, p2, p3, p4]
    slot = scal[2]
    w_of = stream(scal[0], slot, w_ref, held, sems)
    later = jnp.minimum(slot + 1, w_ref.shape[1] - 1)
    ahead = [
        pltpu.make_async_copy(w_ref.at[:, slot, QKV_ROWS:ALL_ROWS, :], wout_ref, sems.at[SN]),
        pltpu.make_async_copy(w_ref.at[:, later, Q_ROWS:QKV_ROWS, :], wkv_ref, sems.at[SN + 1]),
    ]
    for copy in ahead:
        copy.start()
    q_ref[...] = project(scal[0], gain_ref, scal[3], refs, w_of)
    place(scal[0], scal[3], refs, out_ref, out_sems)
    for copy in ahead:
        copy.wait()


def first_keys_kernel(scal, gain_ref, p0, p1, p2, p3, p4, w0, w1, w2, w3, kv_ref, held):
    w_of = assembled(scal[0], scal[1], [w0, w1, w2, w3], held, Q_ROWS)
    write_keys(project(scal[0], gain_ref, scal[3], [p0, p1, p2, p3, p4], w_of), kv_ref)


def first_queries_kernel(scal, gain_ref, p0, p1, p2, p3, p4, w0, w1, w2, w3, q_ref, held):
    w_of = assembled(scal[0], scal[1], [w0, w1, w2, w3], held, 0)
    q_ref[...] = project(scal[0], gain_ref, scal[3], [p0, p1, p2, p3, p4], w_of)


def attend_kernel(scal, q_ref, k_ref, o_ref, *, d, blocks, tok):
    seq = scal[1]
    x_me = jnp.bitwise_and(seq, XN - 1)
    span = ZN * tok
    rows = SHARE * tok
    row = lax.rem(lax.broadcasted_iota(jnp.int32, (rows, 1), 0), tok)
    col = lax.broadcasted_iota(jnp.int32, (1, span), 1)
    col = lax.div(col, tok) * (XN * tok) + lax.rem(col, tok)
    asker = seq - x_me + jnp.bitwise_xor(x_me, d)
    visible = col <= row + (asker - x_me) * tok
    factor = HD**-0.5 * LOG2E
    q_parts = []
    for b in range(blocks):
        q_rows = q_ref[b * tok : (b + 1) * tok, :]
        q_parts += [q_rows[:, h * HD : (h + 1) * HD] for h in range(SHARE)]
    q_rows = jnp.concatenate(q_parts, axis=0)
    q_rows = jnp.concatenate([q_rows, jnp.zeros((blocks * rows, HD), BF16)], axis=1)
    pairs = []
    scores = {}
    for kb in range(blocks):
        pair = k_ref[:, kb * tok : (kb + 1) * tok, :].reshape(span, 2 * HD)
        s = lax.dot_general(
            q_rows[kb * rows :], pair, (((1,), (1,)), ((), ())), preferred_element_type=F32
        )
        pairs.append(pair)
        for b in range(kb, blocks):
            part = s[(b - kb) * rows : (b - kb + 1) * rows]
            scores[b, kb] = jnp.where(visible, part, NEG) if b == kb else part
    peaks = []
    for b in range(blocks):
        peak = functools.reduce(jnp.maximum, [scores[b, kb] for kb in range(b + 1)])
        peaks.append(jnp.max(peak, axis=-1, keepdims=True) * factor)
    totals = [jnp.zeros((rows, span), F32) for _ in range(blocks)]
    sums = [jnp.zeros((rows, 2 * HD), F32) for _ in range(blocks)]
    for kb in range(blocks):
        probs = []
        for b in range(kb, blocks):
            p = jnp.exp2(scores[b, kb] * factor - peaks[b])
            totals[b] += p
            probs.append(p.astype(BF16))
        got = jnp.dot(jnp.concatenate(probs, axis=0), pairs[kb], preferred_element_type=F32)
        for b in range(kb, blocks):
            sums[b] += got[(b - kb) * rows : (b - kb + 1) * rows]
    lane = lax.broadcasted_iota(jnp.int32, (tok, 2 * HD), 1)
    for b in range(blocks):
        total = jnp.sum(totals[b], axis=-1, keepdims=True)
        result = (sums[b][:, HD:] / total).astype(BF16)
        weight = peaks[b] + jnp.log(total) * LOG2E
        high = weight.astype(BF16).astype(F32)
        low = weight - high
        notes = jnp.zeros((tok, 2 * HD), F32)
        for h in range(SHARE):
            part = slice(h * tok, (h + 1) * tok)
            notes = jnp.where(lane == h, high[part], notes)
            notes = jnp.where(lane == SHARE + h, low[part], notes)
        o_ref[b * tok : (b + 1) * tok, :] = jnp.concatenate(
            [result[h * tok : (h + 1) * tok] for h in range(SHARE)] + [notes.astype(BF16)], axis=1
        )


def combine_kernel(scal, o0, o1, o2, o3, a_ref):
    refs = [o0, o1, o2, o3]
    tile = 2 * HD
    notes = [o_ref[:, QW:].astype(F32) for o_ref in refs]
    weights = [n + pltpu.roll(n, tile - SHARE, 1) for n in notes]
    peak = functools.reduce(jnp.maximum, weights)
    weights = [jnp.exp2(w - peak) for w in weights]
    total = functools.reduce(jnp.add, weights)
    weights = [w / total for w in weights]
    left = lax.broadcasted_iota(jnp.int32, notes[0].shape, 1) < HD
    for j in range(SHARE // 2):
        cols = slice(j * tile, (j + 1) * tile)
        mixed = None
        for w, o_ref in zip(weights, refs):
            share = jnp.where(left, w[:, 2 * j : 2 * j + 1], w[:, 2 * j + 1 : 2 * j + 2])
            term = share * o_ref[:, cols].astype(F32)
            mixed = term if mixed is None else mixed + term
        a_ref[:, cols] = mixed.astype(BF16)


def output(piece_refs, h_ref, w_of, o_ref):
    total = h_ref[...].astype(F32)
    update = jnp.zeros(total.shape, F32)
    for i, (_, value) in enumerate(in_order(piece_refs)):
        update += jnp.dot(value, w_of(i), preferred_element_type=F32)
    o_ref[...] = (total + update).astype(BF16)


def output_kernel(scal, a0, a1, a2, a3, a4, h_ref, wout_ref, o_ref):
    output([a0, a1, a2, a3, a4], h_ref, resident(scal[0], wout_ref), o_ref)


def first_output_kernel(scal, a0, a1, a2, a3, a4, h_ref, w0, w1, w2, w3, o_ref, held):
    w_of = assembled(scal[0], scal[1], [w0, w1, w2, w3], held, 0)
    output([a0, a1, a2, a3, a4], h_ref, w_of, o_ref)


VMEM = pl.BlockSpec(memory_space=pltpu.VMEM)
SMEM = pl.BlockSpec(memory_space=pltpu.SMEM)
ANY = pl.BlockSpec(memory_space=pl.ANY)


def call(kernel, scal, args, out_shape, flops, bytes_accessed, exps=0, scratch=(), big=(), own=None):
    outs = out_shape if isinstance(out_shape, list) else [out_shape]
    in_specs = [SMEM] + [ANY if i in big else VMEM for i in range(len(args))]
    out_specs = [VMEM] * len(outs)
    aliases = {}
    if own is not None:
        out_specs[own[1]] = ANY
        aliases = {own[0] + 1: own[1]}
    single = not isinstance(out_shape, list)
    return pl.pallas_call(
        kernel,
        out_shape=out_shape,
        in_specs=in_specs,
        out_specs=out_specs[0] if single else out_specs,
        scratch_shapes=list(scratch),
        input_output_aliases=aliases,
        compiler_params=pltpu.CompilerParams(vmem_limit_bytes=24 * 1024 * 1024),
        cost_estimate=pl.CostEstimate(flops=flops, bytes_accessed=bytes_accessed, transcendentals=exps),
    )(scal, *args)


def local(inputs, norm_gain, w_query, w_key, w_value, w_out):
    blocks, tok, width = inputs.shape
    rows = blocks * tok
    me = lax.axis_index("section")
    seq = lax.axis_index("seq")
    layers = lax.axis_size("section")
    shard = w_query.shape[1]
    assert shard == SHARD

    def panels(w):
        w = w.reshape(shard, SN, -1, 128)
        return w.transpose(1, 2, 0, 3).reshape(SN, -1, 128)

    pair = jnp.concatenate([w_key[0].reshape(shard, SN, HD), w_value[0].reshape(shard, SN, HD)], axis=-1)
    gain_rows = jnp.broadcast_to(norm_gain.reshape(1, width // 128, 128), (SN, width // 128, 128))
    mine = jnp.concatenate([panels(w_query[0]), panels(pair), panels(w_out[0]), gain_rows], axis=1)
    by_layer = lax.all_to_all(mine, "section", split_axis=0, concat_axis=0, tiled=True)
    gains = by_layer[:, ALL_ROWS:].reshape(layers, SN, 1, QW)
    by_layer = by_layer[:, :ALL_ROWS]

    with jax.named_scope("weights"):
        early = lax.all_gather(by_layer[1:4], "seq", axis=0)
        late = lax.all_gather(by_layer[4:], "seq", axis=0)

        def over_z(part):
            part = jnp.broadcast_to(part[None], (ZN,) + part.shape)
            return lax.all_to_all(
                part, "seq", split_axis=0, concat_axis=0, tiled=True, axis_index_groups=along_z()
            )

        def over_x(part):
            return [part] + [lax.ppermute(part, "seq", seq_pairs(d)) for d in (1, 2, 3)]

        first_qkv = over_z(by_layer[0, :QKV_ROWS])
        first_qkv, first_out = lax.optimization_barrier((first_qkv, by_layer[0, QKV_ROWS:]))
        first_qkv, first_out = lax.optimization_barrier((over_x(first_qkv), over_z(first_out)))
        first_out = over_x(first_out)

    flat = inputs.reshape(rows, width)

    def input_piece(mask):
        return lax.dynamic_slice_in_dim(flat, jnp.bitwise_xor(me, mask) * QW, QW, 1)

    pieces = [input_piece(2 * d) for d in range(4)]
    pieces.append(jnp.stack([input_piece(2 * d + 1) for d in range(4)]))

    piece_shape = jax.ShapeDtypeStruct((rows, QW), BF16)
    kv_shape = jax.ShapeDtypeStruct((ZN, rows, 2 * HD), BF16)
    part_shape = jax.ShapeDtypeStruct((rows, QW + 2 * HD), BF16)
    out_shape = jax.ShapeDtypeStruct((rows, width), BF16)
    seq_keys = ZN * XN * tok
    keys_cost = (4 * rows * width * HD, 2 * (width * 2 * HD + rows * width))
    full_cost = (2 * rows * width * QW, 2 * (width * QW + rows * width))

    def first_room(count):
        return [pltpu.VMEM((XN, ZN, count, 128), BF16)]

    def exchange(q, kv):
        with jax.named_scope("exchange"):
            qs = [lax.ppermute(q, "seq", seq_pairs(d)) for d in (3, 2, 1)]
            qs[0], qs[1] = lax.optimization_barrier((qs[0], qs[1]))
            qs[1], qs[2] = lax.optimization_barrier((qs[1], qs[2]))
            qs = [q] + qs[::-1]
            kv = lax.all_to_all(
                kv, "seq", split_axis=0, concat_axis=0, tiled=True, axis_index_groups=along_z()
            )
        return qs, kv

    def attend(scal, qs, kv):
        parts = [None] * XN
        with jax.named_scope("attend"):
            for d in (3, 2, 1, 0):
                part = call(
                    functools.partial(attend_kernel, d=d, blocks=blocks, tok=tok),
                    scal,
                    (qs[d], kv),
                    part_shape,
                    SHARE * tok * seq_keys * 128 * 6,
                    2 * (ZN * rows * 128 + 3 * rows * QW),
                    SHARE * tok * seq_keys * 6 // 4,
                )
                parts[d] = lax.ppermute(part, "seq", seq_pairs(d)) if d else part
            attended = call(
                combine_kernel,
                scal,
                parts,
                piece_shape,
                10 * rows * QW,
                10 * rows * QW,
            )
            return spread(attended)

    def numbers(slot, layer):
        return jnp.stack([jnp.asarray(v, jnp.int32) for v in (me, seq, slot, layer)])

    scal = numbers(0, 0)
    with jax.named_scope("project"):
        args = (gains, *pieces, *first_qkv)
        kv = call(first_keys_kernel, scal, args, kv_shape, *keys_cost, scratch=first_room(SHARD))
        q = call(first_queries_kernel, scal, args, piece_shape, *full_cost, scratch=first_room(Q_ROWS))
    qs, kv = exchange(q, kv)
    kv, first_out = lax.optimization_barrier((kv, first_out))
    heads = attend(scal, qs, kv)
    with jax.named_scope("output"):
        args = (*heads, pieces[0], *first_out)
        own = call(first_output_kernel, scal, args, piece_shape, *full_cost, scratch=first_room(Q_ROWS))
        pieces = spread(own)
    out = jnp.zeros((rows, width), BF16)

    wkv_shape = jax.ShapeDtypeStruct((ZN * XN, SHARD, 128), BF16)
    wout_shape = jax.ShapeDtypeStruct((ZN * XN, Q_ROWS, 128), BF16)
    query_room = [
        pltpu.VMEM((SN, XN, Q_ROWS, 128), BF16),
        pltpu.SemaphoreType.DMA((SN + 2,)),
        pltpu.SemaphoreType.DMA((SN,)),
    ]

    def step(group, first_layer):
        def body(layer, carry):
            pieces, out, wkv = carry
            scal = numbers(layer - first_layer, layer)
            with jax.named_scope("project"):
                kv = call(keys_kernel, scal, (gains, *pieces, wkv), kv_shape, *keys_cost)
                q, out, wout, wkv = call(
                    queries_kernel,
                    scal,
                    (gains, *pieces, group, out),
                    [piece_shape, out_shape, wout_shape, wkv_shape],
                    *full_cost,
                    scratch=query_room,
                    big=(6, 7),
                    own=(7, 1),
                )
            heads = attend(scal, *exchange(q, kv))
            with jax.named_scope("output"):
                own = call(output_kernel, scal, (*heads, pieces[0], wout), piece_shape, *full_cost)
                return spread(own), out, wkv

        return body

    for group, begin, end in ((early, 1, 4), (late, 4, layers)):
        group, pieces = lax.optimization_barrier((group, pieces))
        carry = (pieces, out, group[:, 0, Q_ROWS:QKV_ROWS])
        pieces, out, _ = lax.fori_loop(begin, end, step(group, begin), carry)
    out = call(
        place_kernel,
        numbers(0, layers),
        (*pieces, out),
        out_shape,
        0,
        4 * rows * width,
        scratch=[pltpu.SemaphoreType.DMA((SN,))],
        big=(5,),
        own=(5, 0),
    )
    return out.reshape(1, blocks, tok, width)


def solution(mesh):
    in_specs = (
        P(None, "seq", None),
        P("section", None),
        P("section", "seq", None),
        P("section", "seq", None),
        P("section", "seq", None),
        P("section", "seq", None),
    )
    out_specs = P("section", None, "seq", None)
    return jax.shard_map(local, mesh=mesh, in_specs=in_specs, out_specs=out_specs, check_vma=False)
```

```python
import functools

import jax
import jax.numpy as jnp
from jax import lax
from jax.experimental import pallas as pl
from jax.experimental.pallas import tpu as pltpu
from jax.sharding import PartitionSpec as P

HEADS = 32
KVH = 8
HD = 64
SHARE = HEADS // KVH
QW = SHARE * HD
EPS = 1e-05
NEG = -1e30
LOG2E = 1.4426950408889634
SHARD = 64
Q_ROWS = QW // 128 * SHARD
QKV_ROWS = Q_ROWS + SHARD
ALL_ROWS = QKV_ROWS + Q_ROWS

ZN = 8
XN = 4
SN = 8
F32 = jnp.float32
BF16 = jnp.bfloat16


def seq_pairs(mask):
    return [(i, i ^ mask) for i in range(ZN * XN)]


def section_pairs(mask):
    return [(i, i ^ mask) for i in range(SN)]


def along_z():
    return [[z * XN + x for z in range(ZN)] for x in range(XN)]


def spread(piece):
    near = [piece] + [lax.ppermute(piece, "section", section_pairs(2 * d)) for d in (1, 2, 3)]
    other = lax.ppermute(jnp.stack(near), "section", section_pairs(1))
    return near + [other]


def in_order(refs):
    out = [(2 * d, refs[d][...]) for d in range(4)]
    out += [(2 * d + 1, refs[4][d]) for d in range(4)]
    return out


def place(me, layer, piece_refs, out_ref, sems):
    def copies():
        for i, (mask, source) in enumerate(sources(piece_refs)):
            first = pl.multiple_of(jnp.bitwise_xor(me, mask) * QW, QW)
            yield pltpu.make_async_copy(source, out_ref.at[:, pl.ds(first, QW)], sems.at[i])

    @pl.when(me == layer - 1)
    def _():
        for copy in copies():
            copy.start()
        for copy in copies():
            copy.wait()


def sources(refs):
    out = [(2 * d, refs[d]) for d in range(4)]
    return out + [(2 * d + 1, refs[4].at[d]) for d in range(4)]


def place_kernel(scal, p0, p1, p2, p3, p4, out_in, out_ref, sems):
    place(scal[0], scal[3], [p0, p1, p2, p3, p4], out_ref, sems)


ORDER = (0, 2, 4, 6, 1, 3, 5, 7)


def lanes(block):
    panels = block.shape[1] // SHARD
    parts = [block[:, p * SHARD : (p + 1) * SHARD, :].reshape(XN * SHARD, 128) for p in range(panels)]
    return parts[0] if panels == 1 else jnp.concatenate(parts, axis=1)


def stream(me, slot, w_ref, held, sems):
    copies = []
    for i, mask in enumerate(ORDER):
        owner = jnp.bitwise_xor(me, mask)
        source = w_ref.at[pl.ds(XN * owner, XN), slot, 0:Q_ROWS, :]
        copies.append(pltpu.make_async_copy(source, held.at[i], sems.at[i]))
    for copy in copies:
        copy.start()

    def w_of(i):
        copies[i].wait()
        return lanes(held[i])

    return w_of


def resident(me, w_ref):
    return lambda i: lanes(w_ref[pl.ds(XN * jnp.bitwise_xor(me, ORDER[i]), XN)])


def assembled(me, seq, parts, held, first):
    x_me = jnp.bitwise_and(seq, XN - 1)
    count = held.shape[2]
    for d in range(XN):
        held[jnp.bitwise_xor(x_me, d)] = parts[d][:, first : first + count, :]
    return lambda i: lanes(held[:, jnp.bitwise_xor(me, ORDER[i])])


def project(me, gain_ref, layer, piece_refs, w_of):
    pieces = [(mask, value.astype(F32)) for mask, value in in_order(piece_refs)]
    width = sum(value.shape[1] for _, value in pieces)
    squares = functools.reduce(jnp.add, [value * value for _, value in pieces])
    scale = lax.rsqrt(jnp.sum(squares, axis=-1, keepdims=True) / width + EPS)
    total = None
    for i, (mask, value) in enumerate(pieces):
        owner = jnp.bitwise_xor(me, mask)
        gain = gain_ref[layer, pl.ds(owner, 1), 0, :].astype(F32)
        normed = (value * scale * gain).astype(BF16)
        part = jnp.dot(normed, w_of(i), preferred_element_type=F32)
        total = part if total is None else total + part
    return total.astype(BF16)


def write_keys(pair, kv_ref):
    for i in range(kv_ref.shape[0]):
        kv_ref[i] = pair


def keys_kernel(scal, gain_ref, p0, p1, p2, p3, p4, wkv_ref, kv_ref):
    w_of = resident(scal[0], wkv_ref)
    write_keys(project(scal[0], gain_ref, scal[3], [p0, p1, p2, p3, p4], w_of), kv_ref)


def queries_kernel(
    scal, gain_ref, p0, p1, p2, p3, p4, w_ref, out_in, q_ref, out_ref, wout_ref, wkv_ref, held, sems, out_sems
):
    refs = [p0, p1, p2, p3, p4]
    slot = scal[2]
    w_of = stream(scal[0], slot, w_ref, held, sems)
    later = jnp.minimum(slot + 1, w_ref.shape[1] - 1)
    ahead = [
        pltpu.make_async_copy(w_ref.at[:, slot, QKV_ROWS:ALL_ROWS, :], wout_ref, sems.at[SN]),
        pltpu.make_async_copy(w_ref.at[:, later, Q_ROWS:QKV_ROWS, :], wkv_ref, sems.at[SN + 1]),
    ]
    for copy in ahead:
        copy.start()
    q_ref[...] = project(scal[0], gain_ref, scal[3], refs, w_of)
    place(scal[0], scal[3], refs, out_ref, out_sems)
    for copy in ahead:
        copy.wait()


def first_keys_kernel(scal, gain_ref, p0, p1, p2, p3, p4, w0, w1, w2, w3, kv_ref, held):
    w_of = assembled(scal[0], scal[1], [w0, w1, w2, w3], held, Q_ROWS)
    write_keys(project(scal[0], gain_ref, scal[3], [p0, p1, p2, p3, p4], w_of), kv_ref)


def first_queries_kernel(scal, gain_ref, p0, p1, p2, p3, p4, w0, w1, w2, w3, q_ref, held):
    w_of = assembled(scal[0], scal[1], [w0, w1, w2, w3], held, 0)
    q_ref[...] = project(scal[0], gain_ref, scal[3], [p0, p1, p2, p3, p4], w_of)


def attend_kernel(scal, q_ref, k_ref, o_ref, *, d, blocks, tok):
    seq = scal[1]
    x_me = jnp.bitwise_and(seq, XN - 1)
    span = ZN * tok
    rows = SHARE * tok
    row = lax.rem(lax.broadcasted_iota(jnp.int32, (rows, 1), 0), tok)
    col = lax.broadcasted_iota(jnp.int32, (1, span), 1)
    col = lax.div(col, tok) * (XN * tok) + lax.rem(col, tok)
    asker = seq - x_me + jnp.bitwise_xor(x_me, d)
    visible = col <= row + (asker - x_me) * tok
    factor = HD**-0.5 * LOG2E
    q_parts = []
    for b in range(blocks):
        q_rows = q_ref[b * tok : (b + 1) * tok, :]
        q_parts += [q_rows[:, h * HD : (h + 1) * HD] for h in range(SHARE)]
    q_rows = jnp.concatenate(q_parts, axis=0)
    q_rows = jnp.concatenate([q_rows, jnp.zeros((blocks * rows, HD), BF16)], axis=1)
    pairs = []
    scores = {}
    for kb in range(blocks):
        pair = k_ref[:, kb * tok : (kb + 1) * tok, :].reshape(span, 2 * HD)
        s = lax.dot_general(
            q_rows[kb * rows :], pair, (((1,), (1,)), ((), ())), preferred_element_type=F32
        )
        pairs.append(pair)
        for b in range(kb, blocks):
            part = s[(b - kb) * rows : (b - kb + 1) * rows]
            scores[b, kb] = jnp.where(visible, part, NEG) if b == kb else part
    peaks = []
    for b in range(blocks):
        peak = functools.reduce(jnp.maximum, [scores[b, kb] for kb in range(b + 1)])
        peaks.append(jnp.max(peak, axis=-1, keepdims=True) * factor)
    totals = [jnp.zeros((rows, span), F32) for _ in range(blocks)]
    sums = [jnp.zeros((rows, 2 * HD), F32) for _ in range(blocks)]
    for kb in range(blocks):
        probs = []
        for b in range(kb, blocks):
            p = jnp.exp2(scores[b, kb] * factor - peaks[b])
            totals[b] += p
            probs.append(p.astype(BF16))
        got = jnp.dot(jnp.concatenate(probs, axis=0), pairs[kb], preferred_element_type=F32)
        for b in range(kb, blocks):
            sums[b] += got[(b - kb) * rows : (b - kb + 1) * rows]
    lane = lax.broadcasted_iota(jnp.int32, (tok, 2 * HD), 1)
    for b in range(blocks):
        total = jnp.sum(totals[b], axis=-1, keepdims=True)
        result = (sums[b][:, HD:] / total).astype(BF16)
        weight = peaks[b] + jnp.log(total) * LOG2E
        high = weight.astype(BF16).astype(F32)
        low = weight - high
        notes = jnp.zeros((tok, 2 * HD), F32)
        for h in range(SHARE):
            part = slice(h * tok, (h + 1) * tok)
            notes = jnp.where(lane == h, high[part], notes)
            notes = jnp.where(lane == SHARE + h, low[part], notes)
        o_ref[b * tok : (b + 1) * tok, :] = jnp.concatenate(
            [result[h * tok : (h + 1) * tok] for h in range(SHARE)] + [notes.astype(BF16)], axis=1
        )


def combine_kernel(scal, o0, o1, o2, o3, a_ref):
    refs = [o0, o1, o2, o3]
    tile = 2 * HD
    notes = [o_ref[:, QW:].astype(F32) for o_ref in refs]
    weights = [n + pltpu.roll(n, tile - SHARE, 1) for n in notes]
    peak = functools.reduce(jnp.maximum, weights)
    weights = [jnp.exp2(w - peak) for w in weights]
    total = functools.reduce(jnp.add, weights)
    weights = [w / total for w in weights]
    left = lax.broadcasted_iota(jnp.int32, notes[0].shape, 1) < HD
    for j in range(SHARE // 2):
        cols = slice(j * tile, (j + 1) * tile)
        mixed = None
        for w, o_ref in zip(weights, refs):
            share = jnp.where(left, w[:, 2 * j : 2 * j + 1], w[:, 2 * j + 1 : 2 * j + 2])
            term = share * o_ref[:, cols].astype(F32)
            mixed = term if mixed is None else mixed + term
        a_ref[:, cols] = mixed.astype(BF16)


def output(piece_refs, h_ref, w_of, o_ref):
    total = h_ref[...].astype(F32)
    update = jnp.zeros(total.shape, F32)
    for i, (_, value) in enumerate(in_order(piece_refs)):
        update += jnp.dot(value, w_of(i), preferred_element_type=F32)
    o_ref[...] = (total + update).astype(BF16)


def output_kernel(scal, a0, a1, a2, a3, a4, h_ref, wout_ref, o_ref):
    output([a0, a1, a2, a3, a4], h_ref, resident(scal[0], wout_ref), o_ref)


def first_output_kernel(scal, a0, a1, a2, a3, a4, h_ref, w0, w1, w2, w3, o_ref, held):
    w_of = assembled(scal[0], scal[1], [w0, w1, w2, w3], held, 0)
    output([a0, a1, a2, a3, a4], h_ref, w_of, o_ref)


VMEM = pl.BlockSpec(memory_space=pltpu.VMEM)
SMEM = pl.BlockSpec(memory_space=pltpu.SMEM)
ANY = pl.BlockSpec(memory_space=pl.ANY)


def call(kernel, scal, args, out_shape, flops, bytes_accessed, exps=0, scratch=(), big=(), own=None):
    outs = out_shape if isinstance(out_shape, list) else [out_shape]
    in_specs = [SMEM] + [ANY if i in big else VMEM for i in range(len(args))]
    out_specs = [VMEM] * len(outs)
    aliases = {}
    if own is not None:
        out_specs[own[1]] = ANY
        aliases = {own[0] + 1: own[1]}
    single = not isinstance(out_shape, list)
    return pl.pallas_call(
        kernel,
        out_shape=out_shape,
        in_specs=in_specs,
        out_specs=out_specs[0] if single else out_specs,
        scratch_shapes=list(scratch),
        input_output_aliases=aliases,
        compiler_params=pltpu.CompilerParams(vmem_limit_bytes=24 * 1024 * 1024),
        cost_estimate=pl.CostEstimate(flops=flops, bytes_accessed=bytes_accessed, transcendentals=exps),
    )(scal, *args)


def local(inputs, norm_gain, w_query, w_key, w_value, w_out):
    blocks, tok, width = inputs.shape
    rows = blocks * tok
    me = lax.axis_index("section")
    seq = lax.axis_index("seq")
    layers = lax.axis_size("section")
    shard = w_query.shape[1]
    assert shard == SHARD

    def panels(w):
        w = w.reshape(shard, SN, -1, 128)
        return w.transpose(1, 2, 0, 3).reshape(SN, -1, 128)

    pair = jnp.concatenate([w_key[0].reshape(shard, SN, HD), w_value[0].reshape(shard, SN, HD)], axis=-1)
    gain_rows = jnp.broadcast_to(norm_gain.reshape(1, width // 128, 128), (SN, width // 128, 128))
    mine = jnp.concatenate([panels(w_query[0]), panels(pair), panels(w_out[0]), gain_rows], axis=1)
    by_layer = lax.all_to_all(mine, "section", split_axis=0, concat_axis=0, tiled=True)
    gains = by_layer[:, ALL_ROWS:].reshape(layers, SN, 1, QW)
    by_layer = by_layer[:, :ALL_ROWS]

    with jax.named_scope("weights"):
        early = lax.all_gather(by_layer[1:4], "seq", axis=0)
        late = lax.all_gather(by_layer[4:], "seq", axis=0)

        def over_z(part):
            part = jnp.broadcast_to(part[None], (ZN,) + part.shape)
            return lax.all_to_all(
                part, "seq", split_axis=0, concat_axis=0, tiled=True, axis_index_groups=along_z()
            )

        def over_x(part):
            return [part] + [lax.ppermute(part, "seq", seq_pairs(d)) for d in (1, 2, 3)]

        first_qkv = over_z(by_layer[0, :QKV_ROWS])
        first_qkv, first_out = lax.optimization_barrier((first_qkv, by_layer[0, QKV_ROWS:]))
        first_qkv, first_out = lax.optimization_barrier((over_x(first_qkv), over_z(first_out)))
        first_out = over_x(first_out)

    flat = inputs.reshape(rows, width)

    def input_piece(mask):
        return lax.dynamic_slice_in_dim(flat, jnp.bitwise_xor(me, mask) * QW, QW, 1)

    pieces = [input_piece(2 * d) for d in range(4)]
    pieces.append(jnp.stack([input_piece(2 * d + 1) for d in range(4)]))

    piece_shape = jax.ShapeDtypeStruct((rows, QW), BF16)
    kv_shape = jax.ShapeDtypeStruct((ZN, rows, 2 * HD), BF16)
    part_shape = jax.ShapeDtypeStruct((rows, QW + 2 * HD), BF16)
    out_shape = jax.ShapeDtypeStruct((rows, width), BF16)
    seq_keys = ZN * XN * tok
    keys_cost = (4 * rows * width * HD, 2 * (width * 2 * HD + rows * width))
    full_cost = (2 * rows * width * QW, 2 * (width * QW + rows * width))

    def first_room(count):
        return [pltpu.VMEM((XN, ZN, count, 128), BF16)]

    def exchange(q, kv):
        with jax.named_scope("exchange"):
            qs = [lax.ppermute(q, "seq", seq_pairs(d)) for d in (3, 2, 1)]
            qs[0], qs[1] = lax.optimization_barrier((qs[0], qs[1]))
            qs[1], qs[2] = lax.optimization_barrier((qs[1], qs[2]))
            qs = [q] + qs[::-1]
            kv = lax.all_to_all(
                kv, "seq", split_axis=0, concat_axis=0, tiled=True, axis_index_groups=along_z()
            )
        return qs, kv

    def attend(scal, qs, kv, held_up=None):
        parts = [None] * XN
        with jax.named_scope("attend"):
            for d in (3, 2, 1, 0):
                part = call(
                    functools.partial(attend_kernel, d=d, blocks=blocks, tok=tok),
                    scal,
                    (qs[d], kv),
                    part_shape,
                    SHARE * tok * seq_keys * 128 * 6,
                    2 * (ZN * rows * 128 + 3 * rows * QW),
                    SHARE * tok * seq_keys * 6 // 4,
                )
                parts[d] = lax.ppermute(part, "seq", seq_pairs(d)) if d else part
            if held_up:
                parts[0], held_up[3] = lax.optimization_barrier((parts[0], held_up[3]))
            attended = call(
                combine_kernel,
                scal,
                parts,
                piece_shape,
                10 * rows * QW,
                10 * rows * QW,
            )
            if held_up:
                attended, held_up[2] = lax.optimization_barrier((attended, held_up[2]))
            return spread(attended)

    def numbers(slot, layer):
        return jnp.stack([jnp.asarray(v, jnp.int32) for v in (me, seq, slot, layer)])

    scal = numbers(0, 0)
    with jax.named_scope("project"):
        args = (gains, *pieces, *first_qkv)
        kv = call(first_keys_kernel, scal, args, kv_shape, *keys_cost, scratch=first_room(SHARD))
        q = call(first_queries_kernel, scal, args, piece_shape, *full_cost, scratch=first_room(Q_ROWS))
    qs, kv = exchange(q, kv)
    kv, first_out[1] = lax.optimization_barrier((kv, first_out[1]))
    heads = attend(scal, qs, kv, first_out)
    with jax.named_scope("output"):
        args = (*heads, pieces[0], *first_out)
        own = call(first_output_kernel, scal, args, piece_shape, *full_cost, scratch=first_room(Q_ROWS))
        pieces = spread(own)
    out = jnp.zeros((rows, width), BF16)

    wkv_shape = jax.ShapeDtypeStruct((ZN * XN, SHARD, 128), BF16)
    wout_shape = jax.ShapeDtypeStruct((ZN * XN, Q_ROWS, 128), BF16)
    query_room = [
        pltpu.VMEM((SN, XN, Q_ROWS, 128), BF16),
        pltpu.SemaphoreType.DMA((SN + 2,)),
        pltpu.SemaphoreType.DMA((SN,)),
    ]

    def step(group, first_layer):
        def body(layer, carry):
            pieces, out, wkv = carry
            scal = numbers(layer - first_layer, layer)
            with jax.named_scope("project"):
                kv = call(keys_kernel, scal, (gains, *pieces, wkv), kv_shape, *keys_cost)
                q, out, wout, wkv = call(
                    queries_kernel,
                    scal,
                    (gains, *pieces, group, out),
                    [piece_shape, out_shape, wout_shape, wkv_shape],
                    *full_cost,
                    scratch=query_room,
                    big=(6, 7),
                    own=(7, 1),
                )
            heads = attend(scal, *exchange(q, kv))
            with jax.named_scope("output"):
                own = call(output_kernel, scal, (*heads, pieces[0], wout), piece_shape, *full_cost)
                return spread(own), out, wkv

        return body

    for group, begin, end in ((early, 1, 4), (late, 4, layers)):
        group, pieces = lax.optimization_barrier((group, pieces))
        carry = (pieces, out, group[:, 0, Q_ROWS:QKV_ROWS])
        pieces, out, _ = lax.fori_loop(begin, end, step(group, begin), carry)
    out = call(
        place_kernel,
        numbers(0, layers),
        (*pieces, out),
        out_shape,
        0,
        4 * rows * width,
        scratch=[pltpu.SemaphoreType.DMA((SN,))],
        big=(5,),
        own=(5, 0),
    )
    return out.reshape(1, blocks, tok, width)


def solution(mesh):
    in_specs = (
        P(None, "seq", None),
        P("section", None),
        P("section", "seq", None),
        P("section", "seq", None),
        P("section", "seq", None),
        P("section", "seq", None),
    )
    out_specs = P("section", None, "seq", None)
    return jax.shard_map(local, mesh=mesh, in_specs=in_specs, out_specs=out_specs, check_vma=False)
```

```python
import functools

import jax
import jax.numpy as jnp
from jax import lax
from jax.experimental import pallas as pl
from jax.experimental.pallas import tpu as pltpu
from jax.sharding import PartitionSpec as P

HEADS = 32
KVH = 8
HD = 64
SHARE = HEADS // KVH
QW = SHARE * HD
EPS = 1e-05
NEG = -1e30
LOG2E = 1.4426950408889634
SHARD = 64
Q_ROWS = QW // 128 * SHARD
QKV_ROWS = Q_ROWS + SHARD
ALL_ROWS = QKV_ROWS + Q_ROWS

ZN = 8
XN = 4
SN = 8
F32 = jnp.float32
BF16 = jnp.bfloat16


def seq_pairs(mask):
    return [(i, i ^ mask) for i in range(ZN * XN)]


def section_pairs(mask):
    return [(i, i ^ mask) for i in range(SN)]


def along_z():
    return [[z * XN + x for z in range(ZN)] for x in range(XN)]


def spread(piece):
    near = [piece] + [lax.ppermute(piece, "section", section_pairs(2 * d)) for d in (1, 2, 3)]
    other = lax.ppermute(jnp.stack(near), "section", section_pairs(1))
    return near + [other]


def in_order(refs):
    out = [(2 * d, refs[d][...]) for d in range(4)]
    out += [(2 * d + 1, refs[4][d]) for d in range(4)]
    return out


def place(me, layer, piece_refs, out_ref, sems):
    def copies():
        for i, (mask, source) in enumerate(sources(piece_refs)):
            first = pl.multiple_of(jnp.bitwise_xor(me, mask) * QW, QW)
            yield pltpu.make_async_copy(source, out_ref.at[:, pl.ds(first, QW)], sems.at[i])

    @pl.when(me == layer - 1)
    def _():
        for copy in copies():
            copy.start()
        for copy in copies():
            copy.wait()


def sources(refs):
    out = [(2 * d, refs[d]) for d in range(4)]
    return out + [(2 * d + 1, refs[4].at[d]) for d in range(4)]


def place_kernel(scal, p0, p1, p2, p3, p4, out_in, out_ref, sems):
    place(scal[0], scal[3], [p0, p1, p2, p3, p4], out_ref, sems)


ORDER = (0, 2, 4, 6, 1, 3, 5, 7)


def lanes(block):
    panels = block.shape[1] // SHARD
    parts = [block[:, p * SHARD : (p + 1) * SHARD, :].reshape(XN * SHARD, 128) for p in range(panels)]
    return parts[0] if panels == 1 else jnp.concatenate(parts, axis=1)


def stream(me, row, w_ref, held, sems):
    copies = []
    for i, mask in enumerate(ORDER):
        owner = jnp.bitwise_xor(me, mask)
        source = w_ref.at[pl.ds(XN * owner, XN), pl.ds(row, Q_ROWS), :]
        copies.append(pltpu.make_async_copy(source, held.at[i], sems.at[i]))
    for copy in copies:
        copy.start()

    def w_of(i):
        copies[i].wait()
        return lanes(held[i])

    return w_of


def resident(me, w_ref):
    return lambda i: lanes(w_ref[pl.ds(XN * jnp.bitwise_xor(me, ORDER[i]), XN)])


def assembled(me, seq, parts, held, first):
    x_me = jnp.bitwise_and(seq, XN - 1)
    count = held.shape[2]
    for d in range(XN):
        held[jnp.bitwise_xor(x_me, d)] = parts[d][:, first : first + count, :]
    return lambda i: lanes(held[:, jnp.bitwise_xor(me, ORDER[i])])


def project(me, gain_ref, layer, piece_refs, w_of):
    pieces = [(mask, value.astype(F32)) for mask, value in in_order(piece_refs)]
    width = sum(value.shape[1] for _, value in pieces)
    squares = functools.reduce(jnp.add, [value * value for _, value in pieces])
    scale = lax.rsqrt(jnp.sum(squares, axis=-1, keepdims=True) / width + EPS)
    total = None
    for i, (mask, value) in enumerate(pieces):
        owner = jnp.bitwise_xor(me, mask)
        gain = gain_ref[layer, pl.ds(owner, 1), 0, :].astype(F32)
        normed = (value * scale * gain).astype(BF16)
        part = jnp.dot(normed, w_of(i), preferred_element_type=F32)
        total = part if total is None else total + part
    return total.astype(BF16)


def write_keys(pair, kv_ref):
    for i in range(kv_ref.shape[0]):
        kv_ref[i] = pair


def keys_kernel(scal, gain_ref, p0, p1, p2, p3, p4, wkv_ref, kv_ref):
    w_of = resident(scal[0], wkv_ref)
    write_keys(project(scal[0], gain_ref, scal[3], [p0, p1, p2, p3, p4], w_of), kv_ref)


def queries_kernel(
    scal, gain_ref, p0, p1, p2, p3, p4, w_ref, out_in, q_ref, out_ref, wout_ref, wkv_ref, held, sems, out_sems
):
    refs = [p0, p1, p2, p3, p4]
    row = pl.multiple_of(scal[2], SHARD)
    w_of = stream(scal[0], row, w_ref, held, sems)
    later = pl.multiple_of(jnp.minimum(row + ALL_ROWS, w_ref.shape[1] - ALL_ROWS), SHARD)
    ahead = [
        pltpu.make_async_copy(w_ref.at[:, pl.ds(row + QKV_ROWS, Q_ROWS), :], wout_ref, sems.at[SN]),
        pltpu.make_async_copy(w_ref.at[:, pl.ds(later + Q_ROWS, SHARD), :], wkv_ref, sems.at[SN + 1]),
    ]
    for copy in ahead:
        copy.start()
    q_ref[...] = project(scal[0], gain_ref, scal[3], refs, w_of)
    place(scal[0], scal[3], refs, out_ref, out_sems)
    for copy in ahead:
        copy.wait()


def first_keys_kernel(scal, gain_ref, p0, p1, p2, p3, p4, w0, w1, w2, w3, kv_ref, held):
    w_of = assembled(scal[0], scal[1], [w0, w1, w2, w3], held, Q_ROWS)
    write_keys(project(scal[0], gain_ref, scal[3], [p0, p1, p2, p3, p4], w_of), kv_ref)


def first_queries_kernel(scal, gain_ref, p0, p1, p2, p3, p4, w0, w1, w2, w3, q_ref, held):
    w_of = assembled(scal[0], scal[1], [w0, w1, w2, w3], held, 0)
    q_ref[...] = project(scal[0], gain_ref, scal[3], [p0, p1, p2, p3, p4], w_of)


def attend_kernel(scal, q_ref, k_ref, o_ref, *, d, blocks, tok):
    seq = scal[1]
    x_me = jnp.bitwise_and(seq, XN - 1)
    span = ZN * tok
    rows = SHARE * tok
    row = lax.rem(lax.broadcasted_iota(jnp.int32, (rows, 1), 0), tok)
    col = lax.broadcasted_iota(jnp.int32, (1, span), 1)
    col = lax.div(col, tok) * (XN * tok) + lax.rem(col, tok)
    asker = seq - x_me + jnp.bitwise_xor(x_me, d)
    visible = col <= row + (asker - x_me) * tok
    factor = HD**-0.5 * LOG2E
    q_parts = []
    for b in range(blocks):
        q_rows = q_ref[b * tok : (b + 1) * tok, :]
        q_parts += [q_rows[:, h * HD : (h + 1) * HD] for h in range(SHARE)]
    q_rows = jnp.concatenate(q_parts, axis=0)
    q_rows = jnp.concatenate([q_rows, jnp.zeros((blocks * rows, HD), BF16)], axis=1)
    pairs = []
    scores = {}
    for kb in range(blocks):
        pair = k_ref[:, kb * tok : (kb + 1) * tok, :].reshape(span, 2 * HD)
        s = lax.dot_general(
            q_rows[kb * rows :], pair, (((1,), (1,)), ((), ())), preferred_element_type=F32
        )
        pairs.append(pair)
        for b in range(kb, blocks):
            part = s[(b - kb) * rows : (b - kb + 1) * rows]
            scores[b, kb] = jnp.where(visible, part, NEG) if b == kb else part
    peaks = []
    for b in range(blocks):
        peak = functools.reduce(jnp.maximum, [scores[b, kb] for kb in range(b + 1)])
        peaks.append(jnp.max(peak, axis=-1, keepdims=True) * factor)
    totals = [jnp.zeros((rows, span), F32) for _ in range(blocks)]
    sums = [jnp.zeros((rows, 2 * HD), F32) for _ in range(blocks)]
    for kb in range(blocks):
        probs = []
        for b in range(kb, blocks):
            p = jnp.exp2(scores[b, kb] * factor - peaks[b])
            totals[b] += p
            probs.append(p.astype(BF16))
        got = jnp.dot(jnp.concatenate(probs, axis=0), pairs[kb], preferred_element_type=F32)
        for b in range(kb, blocks):
            sums[b] += got[(b - kb) * rows : (b - kb + 1) * rows]
    lane = lax.broadcasted_iota(jnp.int32, (tok, 2 * HD), 1)
    for b in range(blocks):
        total = jnp.sum(totals[b], axis=-1, keepdims=True)
        result = (sums[b][:, HD:] / total).astype(BF16)
        weight = peaks[b] + jnp.log(total) * LOG2E
        high = weight.astype(BF16).astype(F32)
        low = weight - high
        notes = jnp.zeros((tok, 2 * HD), F32)
        for h in range(SHARE):
            part = slice(h * tok, (h + 1) * tok)
            notes = jnp.where(lane == h, high[part], notes)
            notes = jnp.where(lane == SHARE + h, low[part], notes)
        o_ref[b * tok : (b + 1) * tok, :] = jnp.concatenate(
            [result[h * tok : (h + 1) * tok] for h in range(SHARE)] + [notes.astype(BF16)], axis=1
        )


def combine_kernel(scal, o0, o1, o2, o3, a_ref):
    refs = [o0, o1, o2, o3]
    tile = 2 * HD
    notes = [o_ref[:, QW:].astype(F32) for o_ref in refs]
    weights = [n + pltpu.roll(n, tile - SHARE, 1) for n in notes]
    peak = functools.reduce(jnp.maximum, weights)
    weights = [jnp.exp2(w - peak) for w in weights]
    total = functools.reduce(jnp.add, weights)
    weights = [w / total for w in weights]
    left = lax.broadcasted_iota(jnp.int32, notes[0].shape, 1) < HD
    for j in range(SHARE // 2):
        cols = slice(j * tile, (j + 1) * tile)
        mixed = None
        for w, o_ref in zip(weights, refs):
            share = jnp.where(left, w[:, 2 * j : 2 * j + 1], w[:, 2 * j + 1 : 2 * j + 2])
            term = share * o_ref[:, cols].astype(F32)
            mixed = term if mixed is None else mixed + term
        a_ref[:, cols] = mixed.astype(BF16)


def output(piece_refs, h_ref, w_of, o_ref):
    total = h_ref[...].astype(F32)
    update = jnp.zeros(total.shape, F32)
    for i, (_, value) in enumerate(in_order(piece_refs)):
        update += jnp.dot(value, w_of(i), preferred_element_type=F32)
    o_ref[...] = (total + update).astype(BF16)


def output_kernel(scal, a0, a1, a2, a3, a4, h_ref, wout_ref, o_ref):
    output([a0, a1, a2, a3, a4], h_ref, resident(scal[0], wout_ref), o_ref)


def first_output_kernel(scal, a0, a1, a2, a3, a4, h_ref, w_ref, o_ref, wkv_ref, held, sems):
    own = pltpu.make_async_copy(w_ref.at[:, 0:Q_ROWS, :], held, sems.at[0])
    ahead = w_ref.at[:, 2 * Q_ROWS : 2 * Q_ROWS + SHARD, :]
    ahead = pltpu.make_async_copy(ahead, wkv_ref, sems.at[1])
    own.start()
    ahead.start()
    own.wait()
    output([a0, a1, a2, a3, a4], h_ref, resident(scal[0], held), o_ref)
    ahead.wait()


VMEM = pl.BlockSpec(memory_space=pltpu.VMEM)
SMEM = pl.BlockSpec(memory_space=pltpu.SMEM)
ANY = pl.BlockSpec(memory_space=pl.ANY)


def call(kernel, scal, args, out_shape, flops, bytes_accessed, exps=0, scratch=(), big=(), own=None):
    outs = out_shape if isinstance(out_shape, list) else [out_shape]
    in_specs = [SMEM] + [ANY if i in big else VMEM for i in range(len(args))]
    out_specs = [VMEM] * len(outs)
    aliases = {}
    if own is not None:
        out_specs[own[1]] = ANY
        aliases = {own[0] + 1: own[1]}
    single = not isinstance(out_shape, list)
    return pl.pallas_call(
        kernel,
        out_shape=out_shape,
        in_specs=in_specs,
        out_specs=out_specs[0] if single else out_specs,
        scratch_shapes=list(scratch),
        input_output_aliases=aliases,
        compiler_params=pltpu.CompilerParams(vmem_limit_bytes=24 * 1024 * 1024),
        cost_estimate=pl.CostEstimate(flops=flops, bytes_accessed=bytes_accessed, transcendentals=exps),
    )(scal, *args)


def local(inputs, norm_gain, w_query, w_key, w_value, w_out):
    blocks, tok, width = inputs.shape
    rows = blocks * tok
    me = lax.axis_index("section")
    seq = lax.axis_index("seq")
    layers = lax.axis_size("section")
    shard = w_query.shape[1]
    assert shard == SHARD

    def panels(w):
        w = w.reshape(shard, SN, -1, 128)
        return w.transpose(1, 2, 0, 3).reshape(SN, -1, 128)

    pair = jnp.concatenate([w_key[0].reshape(shard, SN, HD), w_value[0].reshape(shard, SN, HD)], axis=-1)
    gain_rows = jnp.broadcast_to(norm_gain.reshape(1, width // 128, 128), (SN, width // 128, 128))
    mine = jnp.concatenate([panels(w_query[0]), panels(pair), panels(w_out[0]), gain_rows], axis=1)
    by_layer = lax.all_to_all(mine, "section", split_axis=0, concat_axis=0, tiled=True)
    gains = by_layer[:, ALL_ROWS:].reshape(layers, SN, 1, QW)
    by_layer = by_layer[:, :ALL_ROWS]

    with jax.named_scope("weights"):
        early = jnp.concatenate([by_layer[0, QKV_ROWS:], by_layer[1:4].reshape(-1, 128)])
        early = lax.all_gather(early, "seq", axis=0)
        late = lax.all_gather(by_layer[4:].reshape(-1, 128), "seq", axis=0)

        def over_z(part):
            part = jnp.broadcast_to(part[None], (ZN,) + part.shape)
            return lax.all_to_all(
                part, "seq", split_axis=0, concat_axis=0, tiled=True, axis_index_groups=along_z()
            )

        def over_x(part):
            return [part] + [lax.ppermute(part, "seq", seq_pairs(d)) for d in (1, 2, 3)]

        first_qkv = over_x(over_z(by_layer[0, :QKV_ROWS]))

    flat = inputs.reshape(rows, width)

    def input_piece(mask):
        return lax.dynamic_slice_in_dim(flat, jnp.bitwise_xor(me, mask) * QW, QW, 1)

    pieces = [input_piece(2 * d) for d in range(4)]
    pieces.append(jnp.stack([input_piece(2 * d + 1) for d in range(4)]))

    piece_shape = jax.ShapeDtypeStruct((rows, QW), BF16)
    kv_shape = jax.ShapeDtypeStruct((ZN, rows, 2 * HD), BF16)
    part_shape = jax.ShapeDtypeStruct((rows, QW + 2 * HD), BF16)
    out_shape = jax.ShapeDtypeStruct((rows, width), BF16)
    seq_keys = ZN * XN * tok
    keys_cost = (4 * rows * width * HD, 2 * (width * 2 * HD + rows * width))
    full_cost = (2 * rows * width * QW, 2 * (width * QW + rows * width))

    def first_room(count):
        return [pltpu.VMEM((XN, ZN, count, 128), BF16)]

    def exchange(q, kv):
        with jax.named_scope("exchange"):
            qs = [lax.ppermute(q, "seq", seq_pairs(d)) for d in (3, 2, 1)]
            qs[0], qs[1] = lax.optimization_barrier((qs[0], qs[1]))
            qs[1], qs[2] = lax.optimization_barrier((qs[1], qs[2]))
            qs = [q] + qs[::-1]
            kv = lax.all_to_all(
                kv, "seq", split_axis=0, concat_axis=0, tiled=True, axis_index_groups=along_z()
            )
        return qs, kv

    def attend(scal, qs, kv):
        parts = [None] * XN
        with jax.named_scope("attend"):
            for d in (3, 2, 1, 0):
                part = call(
                    functools.partial(attend_kernel, d=d, blocks=blocks, tok=tok),
                    scal,
                    (qs[d], kv),
                    part_shape,
                    SHARE * tok * seq_keys * 128 * 6,
                    2 * (ZN * rows * 128 + 3 * rows * QW),
                    SHARE * tok * seq_keys * 6 // 4,
                )
                parts[d] = lax.ppermute(part, "seq", seq_pairs(d)) if d else part
            attended = call(
                combine_kernel,
                scal,
                parts,
                piece_shape,
                10 * rows * QW,
                10 * rows * QW,
            )
            return spread(attended)

    def numbers(row, layer):
        return jnp.stack([jnp.asarray(v, jnp.int32) for v in (me, seq, row, layer)])

    wkv_shape = jax.ShapeDtypeStruct((ZN * XN, SHARD, 128), BF16)
    wout_shape = jax.ShapeDtypeStruct((ZN * XN, Q_ROWS, 128), BF16)
    scal = numbers(0, 0)
    with jax.named_scope("project"):
        args = (gains, *pieces, *first_qkv)
        kv = call(first_keys_kernel, scal, args, kv_shape, *keys_cost, scratch=first_room(SHARD))
        q = call(first_queries_kernel, scal, args, piece_shape, *full_cost, scratch=first_room(Q_ROWS))
    qs, kv = exchange(q, kv)
    heads = attend(scal, qs, kv)
    with jax.named_scope("output"):
        own, wkv = call(
            first_output_kernel,
            scal,
            (*heads, pieces[0], early),
            [piece_shape, wkv_shape],
            *full_cost,
            scratch=[pltpu.VMEM(wout_shape.shape, BF16), pltpu.SemaphoreType.DMA((2,))],
            big=(6,),
        )
        pieces = spread(own)
    out = jnp.zeros((rows, width), BF16)

    query_room = [
        pltpu.VMEM((SN, XN, Q_ROWS, 128), BF16),
        pltpu.SemaphoreType.DMA((SN + 2,)),
        pltpu.SemaphoreType.DMA((SN,)),
    ]

    def step(group, first_row, first_layer):
        def body(layer, carry):
            pieces, out, wkv = carry
            scal = numbers(first_row + (layer - first_layer) * ALL_ROWS, layer)
            with jax.named_scope("project"):
                kv = call(keys_kernel, scal, (gains, *pieces, wkv), kv_shape, *keys_cost)
                q, out, wout, wkv = call(
                    queries_kernel,
                    scal,
                    (gains, *pieces, group, out),
                    [piece_shape, out_shape, wout_shape, wkv_shape],
                    *full_cost,
                    scratch=query_room,
                    big=(6, 7),
                    own=(7, 1),
                )
            heads = attend(scal, *exchange(q, kv))
            with jax.named_scope("output"):
                own = call(output_kernel, scal, (*heads, pieces[0], wout), piece_shape, *full_cost)
                return spread(own), out, wkv

        return body

    pieces, out, wkv = lax.fori_loop(1, 4, step(early, Q_ROWS, 1), (pieces, out, wkv))
    late, pieces = lax.optimization_barrier((late, pieces))
    wkv = late[:, Q_ROWS:QKV_ROWS]
    pieces, out, wkv = lax.fori_loop(4, layers, step(late, 0, 4), (pieces, out, wkv))
    out = call(
        place_kernel,
        numbers(0, layers),
        (*pieces, out),
        out_shape,
        0,
        4 * rows * width,
        scratch=[pltpu.SemaphoreType.DMA((SN,))],
        big=(5,),
        own=(5, 0),
    )
    return out.reshape(1, blocks, tok, width)


def solution(mesh):
    in_specs = (
        P(None, "seq", None),
        P("section", None),
        P("section", "seq", None),
        P("section", "seq", None),
        P("section", "seq", None),
        P("section", "seq", None),
    )
    out_specs = P("section", None, "seq", None)
    return jax.shard_map(local, mesh=mesh, in_specs=in_specs, out_specs=out_specs, check_vma=False)
```

```python
import functools

import jax
import jax.numpy as jnp
from jax import lax
from jax.experimental import pallas as pl
from jax.experimental.pallas import tpu as pltpu
from jax.sharding import PartitionSpec as P

HEADS = 32
KVH = 8
HD = 64
SHARE = HEADS // KVH
QW = SHARE * HD
EPS = 1e-05
NEG = -1e30
LOG2E = 1.4426950408889634
SHARD = 64
SPLIT = 3
Q_ROWS = QW // 128 * SHARD
QKV_ROWS = Q_ROWS + SHARD
ALL_ROWS = QKV_ROWS + Q_ROWS

ZN = 8
XN = 4
SN = 8
F32 = jnp.float32
BF16 = jnp.bfloat16


def seq_pairs(mask):
    return [(i, i ^ mask) for i in range(ZN * XN)]


def section_pairs(mask):
    return [(i, i ^ mask) for i in range(SN)]


def along_z():
    return [[z * XN + x for z in range(ZN)] for x in range(XN)]


def spread(piece):
    near = [piece] + [lax.ppermute(piece, "section", section_pairs(2 * d)) for d in (1, 2, 3)]
    other = lax.ppermute(jnp.stack(near), "section", section_pairs(1))
    return near + [other]


def in_order(refs):
    out = [(2 * d, refs[d][...]) for d in range(4)]
    out += [(2 * d + 1, refs[4][d]) for d in range(4)]
    return out


def place(me, layer, piece_refs, out_ref, sems):
    def copies():
        for i, (mask, source) in enumerate(sources(piece_refs)):
            first = pl.multiple_of(jnp.bitwise_xor(me, mask) * QW, QW)
            yield pltpu.make_async_copy(source, out_ref.at[:, pl.ds(first, QW)], sems.at[i])

    @pl.when(me == layer - 1)
    def _():
        for copy in copies():
            copy.start()
        for copy in copies():
            copy.wait()


def sources(refs):
    out = [(2 * d, refs[d]) for d in range(4)]
    return out + [(2 * d + 1, refs[4].at[d]) for d in range(4)]


def place_kernel(scal, p0, p1, p2, p3, p4, out_in, out_ref, sems):
    place(scal[0], scal[3], [p0, p1, p2, p3, p4], out_ref, sems)


ORDER = (0, 2, 4, 6, 1, 3, 5, 7)


def lanes(block):
    panels = block.shape[1] // SHARD
    parts = [block[:, p * SHARD : (p + 1) * SHARD, :].reshape(XN * SHARD, 128) for p in range(panels)]
    return parts[0] if panels == 1 else jnp.concatenate(parts, axis=1)


def stream(me, row, w_ref, held, sems):
    copies = []
    for i, mask in enumerate(ORDER):
        owner = jnp.bitwise_xor(me, mask)
        source = w_ref.at[pl.ds(XN * owner, XN), pl.ds(row, Q_ROWS), :]
        copies.append(pltpu.make_async_copy(source, held.at[i], sems.at[i]))
    for copy in copies:
        copy.start()

    def w_of(i):
        copies[i].wait()
        return lanes(held[i])

    return w_of


def resident(me, w_ref):
    return lambda i: lanes(w_ref[pl.ds(XN * jnp.bitwise_xor(me, ORDER[i]), XN)])


def assembled(me, seq, parts, held, first):
    x_me = jnp.bitwise_and(seq, XN - 1)
    count = held.shape[2]
    for d in range(XN):
        held[jnp.bitwise_xor(x_me, d)] = parts[d][:, first : first + count, :]
    return lambda i: lanes(held[:, jnp.bitwise_xor(me, ORDER[i])])


def project(me, gain_ref, layer, piece_refs, w_of):
    pieces = [(mask, value.astype(F32)) for mask, value in in_order(piece_refs)]
    width = sum(value.shape[1] for _, value in pieces)
    squares = functools.reduce(jnp.add, [value * value for _, value in pieces])
    scale = lax.rsqrt(jnp.sum(squares, axis=-1, keepdims=True) / width + EPS)
    total = None
    for i, (mask, value) in enumerate(pieces):
        owner = jnp.bitwise_xor(me, mask)
        gain = gain_ref[layer, pl.ds(owner, 1), 0, :].astype(F32)
        normed = (value * scale * gain).astype(BF16)
        part = jnp.dot(normed, w_of(i), preferred_element_type=F32)
        total = part if total is None else total + part
    return total.astype(BF16)


def write_keys(pair, kv_ref):
    for i in range(kv_ref.shape[0]):
        kv_ref[i] = pair


def keys_kernel(scal, gain_ref, p0, p1, p2, p3, p4, wkv_ref, kv_ref):
    w_of = resident(scal[0], wkv_ref)
    write_keys(project(scal[0], gain_ref, scal[3], [p0, p1, p2, p3, p4], w_of), kv_ref)


def queries_kernel(
    scal, gain_ref, p0, p1, p2, p3, p4, w_ref, out_in, q_ref, out_ref, wout_ref, wkv_ref, held, sems, out_sems
):
    refs = [p0, p1, p2, p3, p4]
    row = pl.multiple_of(scal[2], SHARD)
    w_of = stream(scal[0], row, w_ref, held, sems)
    later = pl.multiple_of(jnp.minimum(row + ALL_ROWS, w_ref.shape[1] - ALL_ROWS), SHARD)
    ahead = [
        pltpu.make_async_copy(w_ref.at[:, pl.ds(row + QKV_ROWS, Q_ROWS), :], wout_ref, sems.at[SN]),
        pltpu.make_async_copy(w_ref.at[:, pl.ds(later + Q_ROWS, SHARD), :], wkv_ref, sems.at[SN + 1]),
    ]
    for copy in ahead:
        copy.start()
    q_ref[...] = project(scal[0], gain_ref, scal[3], refs, w_of)
    place(scal[0], scal[3], refs, out_ref, out_sems)
    for copy in ahead:
        copy.wait()


def first_keys_kernel(scal, gain_ref, p0, p1, p2, p3, p4, w0, w1, w2, w3, kv_ref, held):
    w_of = assembled(scal[0], scal[1], [w0, w1, w2, w3], held, Q_ROWS)
    write_keys(project(scal[0], gain_ref, scal[3], [p0, p1, p2, p3, p4], w_of), kv_ref)


def first_queries_kernel(scal, gain_ref, p0, p1, p2, p3, p4, w0, w1, w2, w3, q_ref, held):
    w_of = assembled(scal[0], scal[1], [w0, w1, w2, w3], held, 0)
    q_ref[...] = project(scal[0], gain_ref, scal[3], [p0, p1, p2, p3, p4], w_of)


def attend_kernel(scal, q_ref, k_ref, o_ref, *, d, blocks, tok):
    seq = scal[1]
    x_me = jnp.bitwise_and(seq, XN - 1)
    span = ZN * tok
    rows = SHARE * tok
    row = lax.rem(lax.broadcasted_iota(jnp.int32, (rows, 1), 0), tok)
    col = lax.broadcasted_iota(jnp.int32, (1, span), 1)
    col = lax.div(col, tok) * (XN * tok) + lax.rem(col, tok)
    asker = seq - x_me + jnp.bitwise_xor(x_me, d)
    visible = col <= row + (asker - x_me) * tok
    factor = HD**-0.5 * LOG2E
    q_parts = []
    for b in range(blocks):
        q_rows = q_ref[b * tok : (b + 1) * tok, :]
        q_parts += [q_rows[:, h * HD : (h + 1) * HD] for h in range(SHARE)]
    q_rows = jnp.concatenate(q_parts, axis=0)
    q_rows = jnp.concatenate([q_rows, jnp.zeros((blocks * rows, HD), BF16)], axis=1)
    pairs = []
    scores = {}
    for kb in range(blocks):
        pair = k_ref[:, kb * tok : (kb + 1) * tok, :].reshape(span, 2 * HD)
        s = lax.dot_general(
            q_rows[kb * rows :], pair, (((1,), (1,)), ((), ())), preferred_element_type=F32
        )
        pairs.append(pair)
        for b in range(kb, blocks):
            part = s[(b - kb) * rows : (b - kb + 1) * rows]
            scores[b, kb] = jnp.where(visible, part, NEG) if b == kb else part
    peaks = []
    for b in range(blocks):
        peak = functools.reduce(jnp.maximum, [scores[b, kb] for kb in range(b + 1)])
        peaks.append(jnp.max(peak, axis=-1, keepdims=True) * factor)
    totals = [jnp.zeros((rows, span), F32) for _ in range(blocks)]
    sums = [jnp.zeros((rows, 2 * HD), F32) for _ in range(blocks)]
    for kb in range(blocks):
        probs = []
        for b in range(kb, blocks):
            p = jnp.exp2(scores[b, kb] * factor - peaks[b])
            totals[b] += p
            probs.append(p.astype(BF16))
        got = jnp.dot(jnp.concatenate(probs, axis=0), pairs[kb], preferred_element_type=F32)
        for b in range(kb, blocks):
            sums[b] += got[(b - kb) * rows : (b - kb + 1) * rows]
    lane = lax.broadcasted_iota(jnp.int32, (tok, 2 * HD), 1)
    for b in range(blocks):
        total = jnp.sum(totals[b], axis=-1, keepdims=True)
        result = (sums[b][:, HD:] / total).astype(BF16)
        weight = peaks[b] + jnp.log(total) * LOG2E
        high = weight.astype(BF16).astype(F32)
        low = weight - high
        notes = jnp.zeros((tok, 2 * HD), F32)
        for h in range(SHARE):
            part = slice(h * tok, (h + 1) * tok)
            notes = jnp.where(lane == h, high[part], notes)
            notes = jnp.where(lane == SHARE + h, low[part], notes)
        o_ref[b * tok : (b + 1) * tok, :] = jnp.concatenate(
            [result[h * tok : (h + 1) * tok] for h in range(SHARE)] + [notes.astype(BF16)], axis=1
        )


def combine_kernel(scal, o0, o1, o2, o3, a_ref):
    refs = [o0, o1, o2, o3]
    tile = 2 * HD
    notes = [o_ref[:, QW:].astype(F32) for o_ref in refs]
    weights = [n + pltpu.roll(n, tile - SHARE, 1) for n in notes]
    peak = functools.reduce(jnp.maximum, weights)
    weights = [jnp.exp2(w - peak) for w in weights]
    total = functools.reduce(jnp.add, weights)
    weights = [w / total for w in weights]
    left = lax.broadcasted_iota(jnp.int32, notes[0].shape, 1) < HD
    for j in range(SHARE // 2):
        cols = slice(j * tile, (j + 1) * tile)
        mixed = None
        for w, o_ref in zip(weights, refs):
            share = jnp.where(left, w[:, 2 * j : 2 * j + 1], w[:, 2 * j + 1 : 2 * j + 2])
            term = share * o_ref[:, cols].astype(F32)
            mixed = term if mixed is None else mixed + term
        a_ref[:, cols] = mixed.astype(BF16)


def output(piece_refs, h_ref, w_of, o_ref):
    total = h_ref[...].astype(F32)
    update = jnp.zeros(total.shape, F32)
    for i, (_, value) in enumerate(in_order(piece_refs)):
        update += jnp.dot(value, w_of(i), preferred_element_type=F32)
    o_ref[...] = (total + update).astype(BF16)


def output_kernel(scal, a0, a1, a2, a3, a4, h_ref, wout_ref, o_ref):
    output([a0, a1, a2, a3, a4], h_ref, resident(scal[0], wout_ref), o_ref)


def first_output_kernel(scal, a0, a1, a2, a3, a4, h_ref, w_ref, o_ref, wkv_ref, held, sems):
    own = pltpu.make_async_copy(w_ref.at[:, 0:Q_ROWS, :], held, sems.at[0])
    ahead = w_ref.at[:, 2 * Q_ROWS : 2 * Q_ROWS + SHARD, :]
    ahead = pltpu.make_async_copy(ahead, wkv_ref, sems.at[1])
    own.start()
    ahead.start()
    own.wait()
    output([a0, a1, a2, a3, a4], h_ref, resident(scal[0], held), o_ref)
    ahead.wait()


VMEM = pl.BlockSpec(memory_space=pltpu.VMEM)
SMEM = pl.BlockSpec(memory_space=pltpu.SMEM)
ANY = pl.BlockSpec(memory_space=pl.ANY)


def call(kernel, scal, args, out_shape, flops, bytes_accessed, exps=0, scratch=(), big=(), own=None):
    outs = out_shape if isinstance(out_shape, list) else [out_shape]
    in_specs = [SMEM] + [ANY if i in big else VMEM for i in range(len(args))]
    out_specs = [VMEM] * len(outs)
    aliases = {}
    if own is not None:
        out_specs[own[1]] = ANY
        aliases = {own[0] + 1: own[1]}
    single = not isinstance(out_shape, list)
    return pl.pallas_call(
        kernel,
        out_shape=out_shape,
        in_specs=in_specs,
        out_specs=out_specs[0] if single else out_specs,
        scratch_shapes=list(scratch),
        input_output_aliases=aliases,
        compiler_params=pltpu.CompilerParams(vmem_limit_bytes=24 * 1024 * 1024),
        cost_estimate=pl.CostEstimate(flops=flops, bytes_accessed=bytes_accessed, transcendentals=exps),
    )(scal, *args)


def local(inputs, norm_gain, w_query, w_key, w_value, w_out):
    blocks, tok, width = inputs.shape
    rows = blocks * tok
    me = lax.axis_index("section")
    seq = lax.axis_index("seq")
    layers = lax.axis_size("section")
    shard = w_query.shape[1]
    assert shard == SHARD

    def panels(w):
        w = w.reshape(shard, SN, -1, 128)
        return w.transpose(1, 2, 0, 3).reshape(SN, -1, 128)

    pair = jnp.concatenate([w_key[0].reshape(shard, SN, HD), w_value[0].reshape(shard, SN, HD)], axis=-1)
    gain_rows = jnp.broadcast_to(norm_gain.reshape(1, width // 128, 128), (SN, width // 128, 128))
    mine = jnp.concatenate([panels(w_query[0]), panels(pair), panels(w_out[0]), gain_rows], axis=1)
    by_layer = lax.all_to_all(mine, "section", split_axis=0, concat_axis=0, tiled=True)
    gains = by_layer[:, ALL_ROWS:].reshape(layers, SN, 1, QW)
    by_layer = by_layer[:, :ALL_ROWS]

    with jax.named_scope("weights"):
        early = jnp.concatenate([by_layer[0, QKV_ROWS:], by_layer[1:SPLIT].reshape(-1, 128)])
        early = lax.all_gather(early, "seq", axis=0)
        late = lax.all_gather(by_layer[SPLIT:].reshape(-1, 128), "seq", axis=0)

        def over_z(part):
            part = jnp.broadcast_to(part[None], (ZN,) + part.shape)
            return lax.all_to_all(
                part, "seq", split_axis=0, concat_axis=0, tiled=True, axis_index_groups=along_z()
            )

        def over_x(part):
            return [part] + [lax.ppermute(part, "seq", seq_pairs(d)) for d in (1, 2, 3)]

        first_qkv = over_x(over_z(by_layer[0, :QKV_ROWS]))

    flat = inputs.reshape(rows, width)

    def input_piece(mask):
        return lax.dynamic_slice_in_dim(flat, jnp.bitwise_xor(me, mask) * QW, QW, 1)

    pieces = [input_piece(2 * d) for d in range(4)]
    pieces.append(jnp.stack([input_piece(2 * d + 1) for d in range(4)]))

    piece_shape = jax.ShapeDtypeStruct((rows, QW), BF16)
    kv_shape = jax.ShapeDtypeStruct((ZN, rows, 2 * HD), BF16)
    part_shape = jax.ShapeDtypeStruct((rows, QW + 2 * HD), BF16)
    out_shape = jax.ShapeDtypeStruct((rows, width), BF16)
    seq_keys = ZN * XN * tok
    keys_cost = (4 * rows * width * HD, 2 * (width * 2 * HD + rows * width))
    full_cost = (2 * rows * width * QW, 2 * (width * QW + rows * width))

    def first_room(count):
        return [pltpu.VMEM((XN, ZN, count, 128), BF16)]

    def exchange(q, kv):
        with jax.named_scope("exchange"):
            qs = [lax.ppermute(q, "seq", seq_pairs(d)) for d in (3, 2, 1)]
            qs[0], qs[1] = lax.optimization_barrier((qs[0], qs[1]))
            qs[1], qs[2] = lax.optimization_barrier((qs[1], qs[2]))
            qs = [q] + qs[::-1]
            kv = lax.all_to_all(
                kv, "seq", split_axis=0, concat_axis=0, tiled=True, axis_index_groups=along_z()
            )
        return qs, kv

    def attend(scal, qs, kv):
        parts = [None] * XN
        with jax.named_scope("attend"):
            for d in (3, 2, 1, 0):
                part = call(
                    functools.partial(attend_kernel, d=d, blocks=blocks, tok=tok),
                    scal,
                    (qs[d], kv),
                    part_shape,
                    SHARE * tok * seq_keys * 128 * 6,
                    2 * (ZN * rows * 128 + 3 * rows * QW),
                    SHARE * tok * seq_keys * 6 // 4,
                )
                parts[d] = lax.ppermute(part, "seq", seq_pairs(d)) if d else part
            attended = call(
                combine_kernel,
                scal,
                parts,
                piece_shape,
                10 * rows * QW,
                10 * rows * QW,
            )
            return spread(attended)

    def numbers(row, layer):
        return jnp.stack([jnp.asarray(v, jnp.int32) for v in (me, seq, row, layer)])

    wkv_shape = jax.ShapeDtypeStruct((ZN * XN, SHARD, 128), BF16)
    wout_shape = jax.ShapeDtypeStruct((ZN * XN, Q_ROWS, 128), BF16)
    scal = numbers(0, 0)
    with jax.named_scope("project"):
        args = (gains, *pieces, *first_qkv)
        kv = call(first_keys_kernel, scal, args, kv_shape, *keys_cost, scratch=first_room(SHARD))
        q = call(first_queries_kernel, scal, args, piece_shape, *full_cost, scratch=first_room(Q_ROWS))
    qs, kv = exchange(q, kv)
    heads = attend(scal, qs, kv)
    with jax.named_scope("output"):
        own, wkv = call(
            first_output_kernel,
            scal,
            (*heads, pieces[0], early),
            [piece_shape, wkv_shape],
            *full_cost,
            scratch=[pltpu.VMEM(wout_shape.shape, BF16), pltpu.SemaphoreType.DMA((2,))],
            big=(6,),
        )
        pieces = spread(own)
    out = jnp.zeros((rows, width), BF16)

    query_room = [
        pltpu.VMEM((SN, XN, Q_ROWS, 128), BF16),
        pltpu.SemaphoreType.DMA((SN + 2,)),
        pltpu.SemaphoreType.DMA((SN,)),
    ]

    def step(group, first_row, first_layer):
        def body(layer, carry):
            pieces, out, wkv = carry
            scal = numbers(first_row + (layer - first_layer) * ALL_ROWS, layer)
            with jax.named_scope("project"):
                kv = call(keys_kernel, scal, (gains, *pieces, wkv), kv_shape, *keys_cost)
                q, out, wout, wkv = call(
                    queries_kernel,
                    scal,
                    (gains, *pieces, group, out),
                    [piece_shape, out_shape, wout_shape, wkv_shape],
                    *full_cost,
                    scratch=query_room,
                    big=(6, 7),
                    own=(7, 1),
                )
            heads = attend(scal, *exchange(q, kv))
            with jax.named_scope("output"):
                own = call(output_kernel, scal, (*heads, pieces[0], wout), piece_shape, *full_cost)
                return spread(own), out, wkv

        return body

    pieces, out, wkv = lax.fori_loop(1, SPLIT, step(early, Q_ROWS, 1), (pieces, out, wkv))
    late, pieces = lax.optimization_barrier((late, pieces))
    wkv = late[:, Q_ROWS:QKV_ROWS]
    pieces, out, wkv = lax.fori_loop(SPLIT, layers, step(late, 0, SPLIT), (pieces, out, wkv))
    out = call(
        place_kernel,
        numbers(0, layers),
        (*pieces, out),
        out_shape,
        0,
        4 * rows * width,
        scratch=[pltpu.SemaphoreType.DMA((SN,))],
        big=(5,),
        own=(5, 0),
    )
    return out.reshape(1, blocks, tok, width)


def solution(mesh):
    in_specs = (
        P(None, "seq", None),
        P("section", None),
        P("section", "seq", None),
        P("section", "seq", None),
        P("section", "seq", None),
        P("section", "seq", None),
    )
    out_specs = P("section", None, "seq", None)
    return jax.shard_map(local, mesh=mesh, in_specs=in_specs, out_specs=out_specs, check_vma=False)
```
